32 devices in a mesh: dp: 2 (over y), ctx: 4 (over x, core), exp: 4 (over z).
Axes of the slice: x: 2, y: 2, z: 4, core: 2. Of those that a mesh axis runs over, the one named last changes fastest.
Arguments:
- tokens: bfloat16 [4096, 2048], P(('dp', 'ctx', 'exp')), may hold values from -6 to 6
- cotangent: bfloat16 [4096, 2048], P(('dp', 'ctx', 'exp')), may hold values from -6 to 6
- expert_ids: int32 [4096, 1], P(('dp', 'ctx', 'exp')), may hold values from 0 to 7; in each aligned block of 128 rows (0 to 127, 128 to 255, ...) at most 24 rows name the same one
- router_weight: bfloat16 [2048, 8], replicated, may hold values from -0.125 to 0.125
- gate_up: bfloat16 [8, 2048, 1408], P(('dp', 'exp')), may hold values from -0.125 to 0.125
- down_weight: bfloat16 [8, 704, 2048], P(('dp', 'exp')), may hold values from -0.21875 to 0.21875
Outputs:
- moe_out: bfloat16 [4096, 2048], P(('dp', 'ctx', 'exp'))
- token_grad: bfloat16 [4096, 2048], P(('dp', 'ctx', 'exp'))
- router_grad: float32 [2048, 8], replicated
The draws below stay inside these ranges and needn't reach their ends.
Inputs may be any that keep to these rules, and one draw needn't show every extreme that they name: `expert_ids`: each token names 1 different experts; among the 128 tokens of one device (aligned blocks of 128 rows) no expert is named more than 24 times, a bound that some block reaches.
All inputs are finite; a program needn't handle non-finite values.
Results may differ from the reference program's by a relative error of at most 0.0064.
Values may be sent and summed in bfloat16 or wider, within the bound.
A program may use at most 64 MiB of HBM per device.

```python
import math
import jax
import jax.numpy as jnp
import numpy as np
from jax import lax

D = 2048
FF = 704
TOP = 1
TOK_DEV = 128
EXPERTS = 8
CAP = 24
TOKENS = 4096
N_DP = 2
N_CTX = 4
N_EXP = 4


def levels(key, extent, pieces, least, high):
    loudness = 1.0
    for dim, shards_of in pieces:
        draws = jax.random.uniform(jax.random.fold_in(jax.random.fold_in(key, 6), dim), (shards_of,), jnp.float32, least / len(pieces), high / len(pieces))
        loudness = loudness * jnp.repeat(jnp.exp(draws), extent[dim] // shards_of).reshape((-1,) + (1,) * (len(extent) - 1 - dim))
    return loudness


def routed_block(own_key, own, number, rows, number_of, top, most, lean):
    ranking = jax.random.permutation(own_key, number_of)
    heavy_load, ordinary = shares(number_of, rows * top, most, lean, True), shares(number_of, rows * top, most, lean, False)
    places = jnp.arange(number_of)

    def named(lengths, turn):
        used = int((lengths > 0).sum())
        fixed = max(1, used // 4)
        shifted = fixed + (places - fixed + turn * (used - fixed)) % max(1, number_of - fixed)
        return jnp.zeros((number_of,), jnp.int32).at[ranking[jnp.where(places < fixed, places, shifted)]].set(jnp.asarray(lengths, jnp.int32))

    lengths = jnp.where(number % 4 == 0, named(heavy_load, number // 4), named(ordinary, number - number // 4 - 1))
    mixed = jax.random.permutation(jax.random.fold_in(own, 3), number_of)
    source_of, sink = mixed[0:number_of // 2 * 2:2], mixed[1:number_of // 2 * 2:2]
    slack = jnp.minimum(lengths[source_of] - 1, most - lengths[sink]) // 2
    slack = jnp.where((source_of == ranking[0]) | (sink == ranking[0]) | (lengths[sink] == 0), 0, jnp.maximum(slack, 0))
    shifted = jax.random.randint(jax.random.fold_in(own, 4), (number_of // 2,), 0, 1 << 20) % (slack + 1)
    lengths = lengths.at[source_of].add(-shifted).at[sink].add(shifted)
    members = jnp.searchsorted(jnp.cumsum(lengths), jnp.arange(rows * top), side="right").astype(jnp.int32)
    grid = members.reshape(top, rows).T
    grid = grid[jax.random.permutation(jax.random.fold_in(own, 1), rows)]
    turn = jax.random.randint(jax.random.fold_in(own, 2), (rows, 1), 0, top)
    return jnp.take_along_axis(grid, (jnp.arange(top)[None, :] + turn) % top, axis=1)


def shares(count, total, reach, slope, full):
    weights = [(1 << 20) // math.isqrt(standing ** slope) + 1 for standing in range(1, count + 1)]
    largest = reach if full else min(reach, max(-(-total // count), total * weights[0] // sum(weights)))
    least = 1 if total - largest >= count - 1 else 0
    counts, surplus = [largest] + [least] * (count - 1), total - largest - least * (count - 1)
    while surplus > 0:
        movable = [i for i in range(1, count) if counts[i] < largest] or [i for i in range(1, count) if counts[i] < reach]
        whole, left = sum([weights[i] for i in movable]), surplus
        for i in movable:
            extra = min(reach - counts[i], max(1, left * weights[i] // whole), surplus)
            counts[i] = counts[i] + extra
            surplus = surplus - extra
    return np.array(counts)


def normal_values(stream_key, extent, scale, reach, split=(), kind=jnp.bfloat16):
    array = jax.random.normal(stream_key, extent, jnp.float32) * scale
    if len(split) > 0:
        array = levels(stream_key, extent, split, -0.22, 0.18) * array
    return jnp.clip(array, min=-reach, max=reach).astype(kind)


def setup_inputs(seed: int = 0) -> dict:
    key_of = jax.random.split(jax.random.key(seed), 7)
    tokens = normal_values(key_of[0], (TOKENS, D), 1.0, 6.0, ((0, 32),))
    cotangent = normal_values(key_of[1], (TOKENS, D), 1.0, 6.0, ((0, 32),))
    expert_ids_keys = jax.random.split(jax.random.fold_in(key_of[2], 1), TOKENS // TOK_DEV)
    expert_ids_turns = jax.random.permutation(jax.random.fold_in(key_of[2], 3), TOKENS // TOK_DEV)
    expert_ids = jax.vmap(lambda own, number: routed_block(jax.random.fold_in(key_of[2], 2), own, number, TOK_DEV, EXPERTS, TOP, CAP, 2))(expert_ids_keys, expert_ids_turns).reshape((TOKENS, TOP))
    router_weight = normal_values(key_of[3], (D, EXPERTS), D ** -0.5, 0.125)
    gate_up = normal_values(key_of[4], (EXPERTS, D, 2 * FF), D ** -0.5, 0.125, ((0, 8),))
    down_weight = normal_values(key_of[5], (EXPERTS, FF, D), FF ** -0.5, 0.21875, ((0, 8),))
    return {"tokens": tokens, "cotangent": cotangent, "expert_ids": expert_ids, "router_weight": router_weight, "gate_up": gate_up, "down_weight": down_weight}


def expert_rows(inputs, upstream, w_in, w_out):
    hidden_units = w_out.shape[0]
    pre_act = jnp.dot(inputs, w_in, preferred_element_type=jnp.float32)
    gate_pre = pre_act[:, :hidden_units]
    up_pre = pre_act[:, hidden_units:]
    sig_gate = jax.nn.sigmoid(gate_pre)
    activated = gate_pre * sig_gate
    hidden = (activated * up_pre).astype(jnp.bfloat16)
    outputs = jnp.dot(hidden, w_out, preferred_element_type=jnp.float32).astype(jnp.bfloat16)
    back_hidden = lax.dot_general(upstream, w_out, (((1,), (1,)), ((), ())), preferred_element_type=jnp.float32)
    gate_slope = sig_gate * (1.0 + gate_pre * (1.0 - sig_gate))
    back_pre = jnp.concatenate([back_hidden * up_pre * gate_slope, back_hidden * activated], axis=1).astype(jnp.bfloat16)
    back_in = lax.dot_general(back_pre, w_in, (((1,), (1,)), ((), ())), preferred_element_type=jnp.float32).astype(jnp.bfloat16)
    return outputs, back_in


def reference(tokens, cotangent, expert_ids, router_weight, gate_up, down_weight):
    logits = jnp.dot(tokens, router_weight, preferred_element_type=jnp.float32)
    chosen = (expert_ids[:, :, None] == jnp.arange(EXPERTS, dtype=jnp.int32)[None, None, :]).astype(jnp.float32)
    picked = jnp.sum(chosen * logits[:, None, :], axis=2)
    gates = jax.nn.sigmoid(picked)
    flat_ids = expert_ids.reshape(-1)
    flat_gates = gates.reshape(-1)
    bound = N_DP * N_CTX * N_EXP * CAP

    def one_expert(carry, inputs_now):
        moe_acc, grad_acc, logit_acc = carry
        index, w_in, w_out = inputs_now
        member = flat_ids == index
        rows = jnp.nonzero(member, size=bound, fill_value=0)[0].astype(jnp.int32)
        count = jnp.sum(member.astype(jnp.int32))
        valid = (jnp.arange(bound, dtype=jnp.int32) < count).astype(jnp.float32)
        owner = (rows // TOP).astype(jnp.int32)
        row_inputs = tokens[owner]
        cot_rows = cotangent[owner].astype(jnp.float32)
        gate_rows = flat_gates[rows]
        upstream = (gate_rows[:, None] * cot_rows).astype(jnp.bfloat16)
        outputs, back_in = expert_rows(row_inputs, upstream, w_in, w_out)
        out_float = outputs.astype(jnp.float32)
        moe_acc = moe_acc.at[owner].add(valid[:, None] * gate_rows[:, None] * out_float)
        grad_acc = grad_acc.at[owner].add(valid[:, None] * back_in.astype(jnp.float32))
        agreement = jnp.sum(cot_rows * out_float, axis=1)
        logit_acc = logit_acc.at[rows].add(valid * gate_rows * (1.0 - gate_rows) * agreement)
        return (moe_acc, grad_acc, logit_acc), None

    start = (jnp.zeros(tokens.shape, jnp.float32), jnp.zeros(tokens.shape, jnp.float32), jnp.zeros(flat_ids.shape, jnp.float32))
    carry, unused = lax.scan(one_expert, start, (jnp.arange(EXPERTS, dtype=jnp.int32), gate_up, down_weight))
    moe_acc, grad_acc, logit_acc = carry
    moe_out = moe_acc.astype(jnp.bfloat16)
    logit_grad = logit_acc.reshape(gates.shape)
    dense_grad = jnp.sum(chosen * logit_grad[:, :, None], axis=1).astype(jnp.bfloat16)
    router_back = lax.dot_general(dense_grad, router_weight, (((1,), (1,)), ((), ())), preferred_element_type=jnp.float32)
    token_grad = (grad_acc + router_back).astype(jnp.bfloat16)
    router_grad = lax.dot_general(tokens, dense_grad, (((0,), (0,)), ((), ())), preferred_element_type=jnp.float32) / TOKENS
    return moe_out, token_grad, router_grad
```

```python
import functools

import jax
import jax.numpy as jnp
from jax import lax
from jax.experimental import pallas as pl
from jax.experimental.pallas import tpu as pltpu
from jax.sharding import PartitionSpec as P

MESH = pl.DeviceIdType.MESH
F32 = jnp.float32
BF16 = jnp.bfloat16
I32 = jnp.int32
NT = (((1,), (1,)), ((), ()))
AWAY = -(1 << 20)


def plan(n_dp, n_exp):
    half = n_exp // 2
    cut = (half + 1) // 2
    near = [(d, 0, o) for o in range(half) for d in range(n_dp)]
    far_a = [(d, 1, o) for o in range(cut) for d in range(n_dp)]
    far_b = [(d, 1, o) for o in range(cut, half) for d in range(n_dp)]
    return near, far_a, far_b


def layout(n_dp, n_exp, cap, base):
    near, far_a, far_b = plan(n_dp, n_exp)
    slots = near + far_a + far_b
    pooled = base < cap
    offsets, sizes, at = [], [], 2 * cap if pooled else 0
    for _, h, _ in slots:
        offsets.append(at)
        sizes.append(2 * (base if h else cap))
        at += sizes[-1]
    return slots, (len(near), len(far_a), len(far_b)), offsets, sizes, at, pooled


def kernel(n_dp, n_ctx, n_exp, cap, base, total, *refs):
    (tok_hbm, cot_hbm, ids, rw, gu_hbm, dn_hbm, moe_out, grad_out, rg_out, flag_out,
     stacked, send, recv, res, ret, gu, dn, mine, summed, terms, columns,
     w_sem, fwd_send, fwd_recv, ret_send, ret_recv,
     ctx_send, ctx_recv, col_send, col_recv) = refs[:30]
    slots, (n_near, n_far_a, n_far_b), off, size, total_rows, pooled = layout(n_dp, n_exp, cap, base)
    if pooled:
        (pool, pool_ids, my_pool_ids, spread, extra, extra_out, extra_in,
         hop_send, hop_recv, share_send, share_recv, part_send, part_recv) = refs[30:]
    me_dp, me_ctx, me_exp = lax.axis_index("dp"), lax.axis_index("ctx"), lax.axis_index("exp")
    me = me_dp * n_exp + me_exp
    half = n_exp // 2
    count = len(slots)
    own = slots.index((0, 0, 0))
    tokens_here = stacked.shape[0] // 2
    width = stacked.shape[1]
    hidden_units = dn.shape[0]
    experts = rw.shape[0]
    lines = width // 128

    def peer(slot, way):
        d, h, o = slot
        if way < 0:
            d, h, o = (n_dp - d) % n_dp, h, (half - o) % half
        to_dp = lax.rem(me_dp + d, n_dp)
        to_half = lax.rem(me_exp // half + h, 2)
        to_low = lax.rem(lax.rem(me_exp, half) + o, half)
        return to_dp, to_half * half + to_low

    def at(pair):
        return {"dp": pair[0], "ctx": me_ctx, "exp": pair[1]}

    def at_ctx(j):
        return {"dp": me_dp, "ctx": j, "exp": me_exp}

    def remote(source, target, sent, came, where):
        return pltpu.make_async_remote_copy(
            src_ref=source, dst_ref=target, send_sem=sent, recv_sem=came,
            device_id=where, device_id_type=MESH,
        )

    def span(k):
        return pl.ds(off[k], size[k])

    barrier = pltpu.get_barrier_semaphore()
    for k, slot in enumerate(slots):
        if k != own:
            pl.semaphore_signal(barrier, inc=1, device_id=at(peer(slot, 1)), device_id_type=MESH)
    for j in range(1, n_ctx):
        pl.semaphore_signal(
            barrier, inc=1, device_id=at_ctx(lax.rem(me_ctx + j, n_ctx)), device_id_type=MESH
        )
    loads = [
        pltpu.make_async_copy(tok_hbm, stacked.at[pl.ds(0, tokens_here)], w_sem.at[0]),
        pltpu.make_async_copy(cot_hbm, stacked.at[pl.ds(tokens_here, tokens_here)], w_sem.at[1]),
        pltpu.make_async_copy(gu_hbm.at[0], gu, w_sem.at[2]),
        pltpu.make_async_copy(dn_hbm.at[0], dn, w_sem.at[3]),
    ]
    for load in loads:
        load.start()

    ids_row = ids[...]
    r_iota = lax.broadcasted_iota(I32, (tokens_here, tokens_here), 0)
    c_iota = lax.broadcasted_iota(I32, (tokens_here, tokens_here), 1)
    ids_wide = jnp.broadcast_to(ids_row, (tokens_here, tokens_here))
    ids_col = jnp.sum(jnp.where(r_iota == c_iota, ids_wide, 0), axis=1, keepdims=True)
    same = ids_col == ids_row
    rank_row = jnp.sum(jnp.where(same & (r_iota < c_iota), 1, 0), axis=0, keepdims=True)
    rank_col = jnp.sum(jnp.where(same & (c_iota < r_iota), 1, 0), axis=1, keepdims=True)
    place_row, place_col = rank_row, rank_col
    far_row, far_col = jnp.zeros_like(ids_row), jnp.zeros_like(ids_col)
    for k, slot in enumerate(slots):
        to_dp, to_exp = peer(slot, 1)
        expert = to_dp * n_exp + to_exp
        place_row = place_row + jnp.where(ids_row == expert, off[k], 0)
        place_col = place_col + jnp.where(ids_col == expert, off[k], 0)
        if slot[1] and pooled:
            far_row = far_row + jnp.where(ids_row == expert, 1, 0)
            far_col = far_col + jnp.where(ids_col == expert, 1, 0)
    second_row, second_col = place_row + cap, place_col + cap
    if pooled:
        over_row = jnp.where(rank_row >= base, far_row, 0)
        over_col = jnp.where(rank_col >= base, far_col, 0)
        turn_row = jnp.sum(jnp.where(r_iota < c_iota, over_col, 0), axis=0, keepdims=True)
        turn_col = jnp.sum(jnp.where(c_iota < r_iota, over_row, 0), axis=1, keepdims=True)
        spill = jnp.sum(jnp.where(turn_row >= cap, over_row, 0), axis=1, keepdims=True)
        turn_row = jnp.where(turn_row >= cap, AWAY, turn_row)
        turn_col = jnp.where(turn_col >= cap, AWAY, turn_col)
        second_row = jnp.where(over_row == 1, turn_row + cap, place_row + jnp.where(far_row == 1, base, cap))
        second_col = jnp.where(over_col == 1, turn_col + cap, place_col + jnp.where(far_col == 1, base, cap))
        place_row = jnp.where(over_row == 1, turn_row, place_row)
        place_col = jnp.where(over_col == 1, turn_col, place_col)
        here = (turn_col == c_iota) | (turn_col + cap == c_iota)
        named = jnp.where((over_col == 1) & here, ids_col + 1, 0)
        my_pool_ids[...] = jnp.broadcast_to(
            jnp.sum(named, axis=0, keepdims=True).astype(F32), my_pool_ids.shape
        )

    fwd, back = [], []
    for k, slot in enumerate(slots):
        if k == own:
            fwd.append(None)
            back.append(None)
            continue
        fwd.append(remote(send.at[span(k)], recv.at[span(k)], fwd_send.at[k], fwd_recv.at[k],
                          at(peer(slot, 1))))
        back.append(remote(res.at[span(k)], ret.at[span(k)], ret_send.at[k], ret_recv.at[k],
                           at(peer(slot, -1))))
    hops, shares, parts = [], [], []
    more = 2 * (cap - base)
    if pooled:
        block = pl.ds(0, 2 * cap)
        across, home = at(peer((0, 1, 0), 1)), at(peer((0, 1, 0), -1))
        hops = [
            remote(send.at[block], pool, hop_send.at[0], hop_recv.at[0], across),
            remote(my_pool_ids, pool_ids, hop_send.at[1], hop_recv.at[1], across),
            remote(res.at[block], ret.at[block], hop_send.at[2], hop_recv.at[2], home),
        ]
        for j, slot in enumerate(slots[:n_near]):
            if j == own:
                continue
            cut = pl.ds(j * more, more)
            shares.append(remote(spread.at[cut], extra.at[cut], share_send.at[j], share_recv.at[j],
                                 at(peer(slot, 1))))
            parts.append(remote(extra_out.at[cut], extra_in.at[cut], part_send.at[j], part_recv.at[j],
                                at(peer(slot, -1))))

    def pack(first, last):
        spot = lax.broadcasted_iota(I32, (last - first, tokens_here), 0) + first
        pick_tok = jnp.where(spot == place_row, 1.0, 0.0).astype(BF16)
        pick_cot = jnp.where(spot == second_row, 1.0, 0.0).astype(BF16)
        pick = jnp.concatenate([pick_tok, pick_cot], axis=1)
        send[first:last] = jnp.dot(pick, stacked[...], preferred_element_type=F32).astype(BF16)

    loads[0].wait()
    loads[1].wait()
    edges = [n_near, n_near + n_far_a, count]
    groups = [(n_near, edges[1]), (edges[1], count), (0, n_near)]
    waited = False
    if pooled:
        pack(0, 2 * cap)
        pl.semaphore_wait(barrier, count - 1 + n_ctx - 1)
        waited = True
        hops[1].start()
        hops[0].start()
    for first, last in groups:
        if first == last:
            continue
        pack(off[first], off[last - 1] + size[last - 1])
        if not waited:
            pl.semaphore_wait(barrier, count - 1 + n_ctx - 1)
            waited = True
        for k in range(first, last):
            if k != own:
                fwd[k].start()

    row_e = lax.broadcasted_iota(I32, (experts, width), 0)
    router_row = jnp.sum(jnp.where(row_e == me, rw[...].astype(F32), 0.0), axis=0, keepdims=True)

    def expert_pass(x_wide, c_wide):
        m = x_wide.shape[0]
        x = x_wide.astype(BF16)
        logits = lax.dot_general(x, rw[...], NT, preferred_element_type=F32)
        lane = lax.broadcasted_iota(I32, (m, experts), 1)
        gate = jax.nn.sigmoid(jnp.sum(jnp.where(lane == me, logits, 0.0), axis=1, keepdims=True))
        upstream = (gate * c_wide).astype(BF16)
        pre = jnp.dot(x, gu[...], preferred_element_type=F32)
        a = pre[:, :hidden_units]
        u = pre[:, hidden_units:]
        s = jax.nn.sigmoid(a)
        act = a * s
        hidden = (act * u).astype(BF16)
        out = jnp.dot(hidden, dn[...], preferred_element_type=F32).astype(BF16).astype(F32)
        back_hidden = lax.dot_general(upstream, dn[...], NT, preferred_element_type=F32)
        back_pre = jnp.concatenate(
            [back_hidden * u * (s * (1.0 + a * (1.0 - s))), back_hidden * act], axis=1
        ).astype(BF16)
        back_in = lax.dot_general(back_pre, gu[...], NT, preferred_element_type=F32)
        agreement = jnp.sum(c_wide * out, axis=1, keepdims=True)
        dense = (gate * (1.0 - gate) * agreement).astype(BF16).astype(F32)
        moe = gate * out
        grad = back_in.astype(BF16).astype(F32) + dense * router_row
        return moe, grad, jnp.sum(dense * x_wide, axis=0, keepdims=True)

    def slots_pass(first, last, with_extra=False):
        xs, cs = [], []
        for k in range(first, last):
            if k == own:
                block = send[span(k)].astype(F32)
            else:
                fwd[k].wait_recv()
                block = recv[span(k)].astype(F32)
            xs.append(block[:size[k] // 2])
            cs.append(block[size[k] // 2:])
        if with_extra:
            for share in shares:
                share.wait_recv()
            for j in range(n_near):
                source = spread if j == own else extra
                block = source[j * more:(j + 1) * more].astype(F32)
                xs.append(block[:more // 2])
                cs.append(block[more // 2:])
        moe, grad, term = expert_pass(jnp.concatenate(xs, axis=0), jnp.concatenate(cs, axis=0))
        start = 0
        if with_extra:
            start = (last - first) * size[first] // 2
            for j in range(n_near):
                part = slice(start + j * more // 2, start + (j + 1) * more // 2)
                target = extra_in if j == own else extra_out
                target[j * more:(j + 1) * more] = jnp.concatenate([moe[part], grad[part]], axis=0).astype(BF16)
            for copy in parts:
                copy.start()
        each = size[first] // 2
        for i, k in enumerate(range(first, last)):
            part = slice(i * each, (i + 1) * each)
            block = jnp.concatenate([moe[part], grad[part]], axis=0).astype(BF16)
            if k == own:
                ret[span(k)] = block
            else:
                res[span(k)] = block
                back[k].start()
        return term

    if pooled:
        hops[1].wait_recv()
        hops[0].wait_recv()
        wide = 2 * cap
        pr = lax.broadcasted_iota(I32, (wide, wide), 0)
        pc = lax.broadcasted_iota(I32, (wide, wide), 1)
        name_row = pool_ids[0:1, 0:wide]
        name_col = jnp.sum(jnp.where(pr == pc, jnp.broadcast_to(name_row, (wide, wide)), 0.0), axis=1, keepdims=True)
        lane, line = pc[0:1, :], pr[:, 0:1]
        mate = (name_col == name_row) & ((pr >= cap) == (pc >= cap))
        to_row = jnp.sum(jnp.where(mate & (pr < pc), 1, 0), axis=0, keepdims=True)
        to_col = jnp.sum(jnp.where(mate & (pc < pr), 1, 0), axis=1, keepdims=True)
        to_row = to_row + jnp.where(lane >= cap, more // 2, 0) + jnp.where(name_row == 0.0, AWAY, 0)
        to_col = to_col + jnp.where(line >= cap, more // 2, 0) + jnp.where(name_col == 0.0, AWAY, 0)
        for j, slot in enumerate(slots[:n_near]):
            to_dp, to_exp = peer(slot, 1)
            expert = (to_dp * n_exp + to_exp + 1).astype(F32)
            to_row = to_row + jnp.where(name_row == expert, j * more, 0)
            to_col = to_col + jnp.where(name_col == expert, j * more, 0)
        spot = lax.broadcasted_iota(I32, (n_near * more, wide), 0)
        deal = jnp.where(spot == to_row, 1.0, 0.0).astype(BF16)
        spread[...] = jnp.dot(deal, pool[...], preferred_element_type=F32).astype(BF16)
        for share in shares:
            share.start()
    loads[2].wait()
    loads[3].wait()
    router_sum = slots_pass(n_near, edges[1])
    router_sum = router_sum + slots_pass(0, n_near, pooled)
    if pooled:
        for part in parts:
            part.wait_recv()
        spot = lax.broadcasted_iota(I32, (wide, n_near * more), 1)
        gather = jnp.where(spot == to_col, 1.0, 0.0).astype(BF16)
        res[0:wide] = jnp.dot(gather, extra_in[...], preferred_element_type=F32).astype(BF16)
        hops[2].start()
    if n_far_b:
        router_sum = router_sum + slots_pass(edges[1], count)

    router_sum = router_sum * (1.0 / total)
    for i in range(lines):
        mine[i:i + 1, :] = router_sum[:, i * 128:(i + 1) * 128]
    if pooled:
        mine[lines:lines + 8, :] = jnp.broadcast_to(spill.astype(F32), (8, 128))
    terms[me_ctx] = mine[...]
    ctx_copies = []
    for j in range(1, n_ctx):
        copy = remote(mine, terms.at[me_ctx], ctx_send.at[j], ctx_recv.at[me_ctx],
                      at_ctx(lax.rem(me_ctx + j, n_ctx)))
        copy.start()
        ctx_copies.append(copy)
    for j in range(1, n_ctx):
        source = lax.rem(me_ctx + j, n_ctx)
        remote(mine, terms.at[source], ctx_send.at[j], ctx_recv.at[source], at_ctx(source)).wait_recv()
    column = terms[0]
    for j in range(1, n_ctx):
        column = column + terms[j]
    summed[...] = column
    columns[me] = column
    col_copies = []
    for k, slot in enumerate(slots):
        if k != own:
            copy = remote(summed, columns.at[me], col_send.at[k], col_recv.at[me], at(peer(slot, 1)))
            copy.start()
            col_copies.append(copy)

    def unpack(first, last, fresh):
        spot = lax.broadcasted_iota(I32, (tokens_here, last - first), 1) + first
        put_moe = jnp.where(spot == place_col, 1.0, 0.0).astype(BF16)
        put_grad = jnp.where(spot == second_col, 1.0, 0.0).astype(BF16)
        put = jnp.concatenate([put_moe, put_grad], axis=0)
        placed = jnp.dot(put, ret[first:last], preferred_element_type=F32)
        if fresh:
            moe_out[...] = placed[:tokens_here].astype(BF16)
            grad_out[...] = placed[tokens_here:].astype(BF16)
        else:
            moe_out[...] = (moe_out[...].astype(F32) + placed[:tokens_here]).astype(BF16)
            grad_out[...] = (grad_out[...].astype(F32) + placed[tokens_here:]).astype(BF16)

    split = edges[1] if n_far_b else count
    for k in range(split):
        if k != own:
            back[k].wait_recv()
    if pooled:
        hops[2].wait_recv()
    middle = off[split - 1] + size[split - 1]
    unpack(0, middle, True)
    if split < count:
        for k in range(split, count):
            back[k].wait_recv()
        unpack(middle, total_rows, False)

    for k, slot in enumerate(slots):
        if k != own:
            from_dp, from_exp = peer(slot, -1)
            source = from_dp * n_exp + from_exp
            remote(summed, columns.at[source], col_send.at[k], col_recv.at[source],
                   at(peer(slot, -1))).wait_recv()
    for i in range(lines):
        rg_out[:, i * 128:(i + 1) * 128] = columns[:, i, :]
    if pooled:
        flag_out[0, 0] = jnp.max(columns[:, lines:lines + 8, :])
    else:
        flag_out[0, 0] = jnp.float32(0.0)
    for copy in fwd + back + hops + shares + parts:
        if copy is not None:
            copy.wait_send()
    for copy in ctx_copies + col_copies:
        copy.wait_send()


def hand_over(moe, grad, columns, moe_out, grad_out, rg_out, moe_buf, grad_buf, rg_buf, in_sem, out_sem):
    half = moe.shape[0] // 2
    parts = [(columns, rg_buf, rg_out)]
    for source, buffer, target in ((moe, moe_buf, moe_out), (grad, grad_buf, grad_out)):
        for start in (0, half):
            cut = pl.ds(start, half)
            parts.append((source.at[cut], buffer.at[cut], target.at[cut]))
    loads, stores = [], []
    for i, (source, buffer, target) in enumerate(parts):
        loads.append(pltpu.make_async_copy(source, buffer, in_sem.at[i]))
        stores.append(pltpu.make_async_copy(buffer, target, out_sem.at[i]))
    for load in loads:
        load.start()
    for load, store in zip(loads, stores):
        load.wait()
        store.start()
    for store in stores:
        store.wait()


def exchange(shape, base, collective, tokens, cotangent, ids, router, gate_up, down_weight):
    n_dp, n_ctx, n_exp = shape
    tok_count, width = tokens.shape
    experts = router.shape[0]
    hidden_units = down_weight.shape[1]
    cap = capacity(tok_count, experts)
    slots, counts, _, _, total_rows, pooled = layout(n_dp, n_exp, cap, base)
    count, n_near = len(slots), counts[0]
    total = tok_count * n_dp * n_ctx * n_exp
    lines = width // 128 + (8 if pooled else 0)
    vmem = pl.BlockSpec(memory_space=pltpu.VMEM)
    hbm = pl.BlockSpec(memory_space=pl.ANY)
    dma = pltpu.SemaphoreType.DMA
    rows = pltpu.VMEM((total_rows, width), BF16)
    more = pltpu.VMEM((n_near * 2 * (cap - base), width), BF16)
    names = pltpu.VMEM((8, 128), F32)
    scratch = [
        pltpu.VMEM((2 * tok_count, width), BF16),
        rows, rows, rows, rows,
        pltpu.VMEM((width, 2 * hidden_units), BF16),
        pltpu.VMEM((hidden_units, width), BF16),
        pltpu.VMEM((lines, 128), F32),
        pltpu.VMEM((lines, 128), F32),
        pltpu.VMEM((n_ctx, lines, 128), F32),
        pltpu.VMEM((experts, lines, 128), F32),
        dma((4,)),
        dma((count,)), dma((count,)), dma((count,)), dma((count,)),
        dma((n_ctx,)), dma((n_ctx,)),
        dma((count,)), dma((count,)),
    ]
    if pooled:
        scratch += [
            pltpu.VMEM((2 * cap, width), BF16), names, names, more, more, more, more,
            dma((3,)), dma((3,)), dma((n_near,)), dma((n_near,)), dma((n_near,)), dma((n_near,)),
        ]
    flops = 2 * 2 * count * cap * width * 3 * hidden_units
    return pl.pallas_call(
        functools.partial(kernel, n_dp, n_ctx, n_exp, cap, base, total),
        out_shape=(
            jax.ShapeDtypeStruct((tok_count, width), BF16),
            jax.ShapeDtypeStruct((tok_count, width), BF16),
            jax.ShapeDtypeStruct((experts, width), F32),
            jax.ShapeDtypeStruct((1, 1), F32),
        ),
        in_specs=[hbm, hbm, vmem, vmem, hbm, hbm],
        out_specs=(vmem, vmem, vmem, pl.BlockSpec(memory_space=pltpu.SMEM)),
        scratch_shapes=scratch,
        compiler_params=pltpu.CompilerParams(
            collective_id=collective, has_side_effects=True, vmem_limit_bytes=58 * 1024 * 1024
        ),
        cost_estimate=pl.CostEstimate(
            flops=flops, bytes_accessed=12 * 1024 * 1024, transcendentals=0
        ),
    )(tokens, cotangent, ids, router, gate_up, down_weight)


def deliver(moe, grad, columns):
    hbm = pl.BlockSpec(memory_space=pl.ANY)
    dma = pltpu.SemaphoreType.DMA
    return pl.pallas_call(
        hand_over,
        out_shape=tuple(jax.ShapeDtypeStruct(v.shape, v.dtype) for v in (moe, grad, columns)),
        in_specs=[hbm, hbm, hbm],
        out_specs=(hbm, hbm, hbm),
        scratch_shapes=[
            pltpu.VMEM(moe.shape, BF16),
            pltpu.VMEM(grad.shape, BF16),
            pltpu.VMEM(columns.shape, F32),
            dma((5,)),
            dma((5,)),
        ],
    )(moe, grad, columns)


def capacity(tok_count, experts):
    most = min(tok_count, 3 * tok_count // (2 * experts))
    return -(-most // 8) * 8


def per_device(n_dp, n_ctx, n_exp, tokens, cotangent, expert_ids, router_weight, gate_up, down_weight):
    tok_count = tokens.shape[0]
    cap = capacity(tok_count, router_weight.shape[1])
    base = min(cap, -(-(2 * cap // 3) // 8) * 8)
    shape = (n_dp, n_ctx, n_exp)
    args = (tokens, cotangent, expert_ids.reshape(1, tok_count), router_weight.T, gate_up, down_weight)
    moe, grad, columns, spilled = exchange(shape, base, 0, *args)
    if base == cap:
        moe, grad, columns = deliver(moe, grad, columns)
        return moe, grad, columns.T

    def short(moe, grad, columns, *args):
        return deliver(moe, grad, columns)

    def full(moe, grad, columns, *args):
        return deliver(*exchange(shape, cap, 1, *args)[:3])

    moe, grad, columns = lax.cond(spilled[0, 0] > 0.0, full, short, moe, grad, columns, *args)
    return moe, grad, columns.T


def solution(mesh):
    in_specs = (
        P(("dp", "ctx", "exp"), None),
        P(("dp", "ctx", "exp"), None),
        P(("dp", "ctx", "exp"), None),
        P(),
        P(("dp", "exp"), None, None),
        P(("dp", "exp"), None, None),
    )
    out_specs = (P(("dp", "ctx", "exp"), None), P(("dp", "ctx", "exp"), None), P())
    shape = mesh.shape
    return jax.shard_map(
        functools.partial(per_device, shape["dp"], shape["ctx"], shape["exp"]),
        mesh=mesh, in_specs=in_specs, out_specs=out_specs, check_vma=False,
    )
```

```python
import functools

import jax
import jax.numpy as jnp
from jax import lax
from jax.experimental import pallas as pl
from jax.experimental.pallas import tpu as pltpu
from jax.sharding import PartitionSpec as P

MESH = pl.DeviceIdType.MESH
F32 = jnp.float32
BF16 = jnp.bfloat16
I32 = jnp.int32
NT = (((1,), (1,)), ((), ()))
AWAY = -(1 << 20)


def plan(n_dp, n_exp):
    half = n_exp // 2
    cut = (half + 1) // 2
    near = [(d, 0, o) for o in range(half) for d in range(n_dp)]
    far_a = [(d, 1, o) for o in range(cut) for d in range(n_dp)]
    far_b = [(d, 1, o) for o in range(cut, half) for d in range(n_dp)]
    return near, far_a, far_b


def layout(n_dp, n_exp, cap, base):
    near, far_a, far_b = plan(n_dp, n_exp)
    slots = near + far_a + far_b
    pooled = base < cap
    offsets, sizes, at = [], [], 2 * cap if pooled else 0
    for _, h, _ in slots:
        offsets.append(at)
        sizes.append(2 * (base if h else cap))
        at += sizes[-1]
    return slots, (len(near), len(far_a), len(far_b)), offsets, sizes, at, pooled


def kernel(n_dp, n_ctx, n_exp, cap, base, total, *refs):
    (tok_hbm, cot_hbm, ids, rw, gu_hbm, dn_hbm, moe_out, grad_out, rg_out, flag_out,
     stacked, send, recv, res, ret, gu, dn, mine, summed, terms, columns,
     w_sem, fwd_send, fwd_recv, ret_send, ret_recv,
     ctx_send, ctx_recv, col_send, col_recv, all_send, all_recv) = refs[:32]
    slots, (n_near, n_far_a, n_far_b), off, size, total_rows, pooled = layout(n_dp, n_exp, cap, base)
    if pooled:
        (pool, pool_ids, my_pool_ids, spread, extra, extra_out, extra_in,
         hop_send, hop_recv, share_send, share_recv, part_send, part_recv) = refs[32:]
    me_dp, me_ctx, me_exp = lax.axis_index("dp"), lax.axis_index("ctx"), lax.axis_index("exp")
    me = me_dp * n_exp + me_exp
    half = n_exp // 2
    count = len(slots)
    own = slots.index((0, 0, 0))
    tokens_here = stacked.shape[0] // 2
    width = stacked.shape[1]
    hidden_units = dn.shape[0]
    experts = rw.shape[0]
    per = width // 128 // n_ctx

    def peer(slot, way):
        d, h, o = slot
        if way < 0:
            d, h, o = (n_dp - d) % n_dp, h, (half - o) % half
        to_dp = lax.rem(me_dp + d, n_dp)
        to_half = lax.rem(me_exp // half + h, 2)
        to_low = lax.rem(lax.rem(me_exp, half) + o, half)
        return to_dp, to_half * half + to_low

    def at(pair):
        return {"dp": pair[0], "ctx": me_ctx, "exp": pair[1]}

    def at_ctx(j):
        return {"dp": me_dp, "ctx": j, "exp": me_exp}

    def remote(source, target, sent, came, where):
        return pltpu.make_async_remote_copy(
            src_ref=source, dst_ref=target, send_sem=sent, recv_sem=came,
            device_id=where, device_id_type=MESH,
        )

    def span(k):
        return pl.ds(off[k], size[k])

    barrier = pltpu.get_barrier_semaphore()
    for k, slot in enumerate(slots):
        if k != own:
            pl.semaphore_signal(barrier, inc=1, device_id=at(peer(slot, 1)), device_id_type=MESH)
    for j in range(1, n_ctx):
        pl.semaphore_signal(
            barrier, inc=1, device_id=at_ctx(lax.rem(me_ctx + j, n_ctx)), device_id_type=MESH
        )
    loads = [
        pltpu.make_async_copy(tok_hbm, stacked.at[pl.ds(0, tokens_here)], w_sem.at[0]),
        pltpu.make_async_copy(cot_hbm, stacked.at[pl.ds(tokens_here, tokens_here)], w_sem.at[1]),
        pltpu.make_async_copy(gu_hbm.at[0], gu, w_sem.at[2]),
        pltpu.make_async_copy(dn_hbm.at[0], dn, w_sem.at[3]),
    ]
    for load in loads:
        load.start()

    ids_row = ids[...]
    r_iota = lax.broadcasted_iota(I32, (tokens_here, tokens_here), 0)
    c_iota = lax.broadcasted_iota(I32, (tokens_here, tokens_here), 1)
    ids_wide = jnp.broadcast_to(ids_row, (tokens_here, tokens_here))
    ids_col = jnp.sum(jnp.where(r_iota == c_iota, ids_wide, 0), axis=1, keepdims=True)
    same = ids_col == ids_row
    rank_row = jnp.sum(jnp.where(same & (r_iota < c_iota), 1, 0), axis=0, keepdims=True)
    rank_col = jnp.sum(jnp.where(same & (c_iota < r_iota), 1, 0), axis=1, keepdims=True)
    place_row, place_col = rank_row, rank_col
    far_row, far_col = jnp.zeros_like(ids_row), jnp.zeros_like(ids_col)
    for k, slot in enumerate(slots):
        to_dp, to_exp = peer(slot, 1)
        expert = to_dp * n_exp + to_exp
        place_row = place_row + jnp.where(ids_row == expert, off[k], 0)
        place_col = place_col + jnp.where(ids_col == expert, off[k], 0)
        if slot[1] and pooled:
            far_row = far_row + jnp.where(ids_row == expert, 1, 0)
            far_col = far_col + jnp.where(ids_col == expert, 1, 0)
    second_row, second_col = place_row + cap, place_col + cap
    if pooled:
        over_row = jnp.where(rank_row >= base, far_row, 0)
        over_col = jnp.where(rank_col >= base, far_col, 0)
        turn_row = jnp.sum(jnp.where(r_iota < c_iota, over_col, 0), axis=0, keepdims=True)
        turn_col = jnp.sum(jnp.where(c_iota < r_iota, over_row, 0), axis=1, keepdims=True)
        spill = jnp.sum(jnp.where(turn_row >= cap, over_row, 0), axis=1, keepdims=True)
        turn_row = jnp.where(turn_row >= cap, AWAY, turn_row)
        turn_col = jnp.where(turn_col >= cap, AWAY, turn_col)
        second_row = jnp.where(over_row == 1, turn_row + cap, place_row + jnp.where(far_row == 1, base, cap))
        second_col = jnp.where(over_col == 1, turn_col + cap, place_col + jnp.where(far_col == 1, base, cap))
        place_row = jnp.where(over_row == 1, turn_row, place_row)
        place_col = jnp.where(over_col == 1, turn_col, place_col)
        here = (turn_col == c_iota) | (turn_col + cap == c_iota)
        named = jnp.where((over_col == 1) & here, ids_col + 1, 0)
        my_pool_ids[...] = jnp.broadcast_to(
            jnp.sum(named, axis=0, keepdims=True).astype(F32), my_pool_ids.shape
        )

    fwd, back = [], []
    for k, slot in enumerate(slots):
        if k == own:
            fwd.append(None)
            back.append(None)
            continue
        fwd.append(remote(send.at[span(k)], recv.at[span(k)], fwd_send.at[k], fwd_recv.at[k],
                          at(peer(slot, 1))))
        back.append(remote(res.at[span(k)], ret.at[span(k)], ret_send.at[k], ret_recv.at[k],
                           at(peer(slot, -1))))
    hops, shares, parts = [], [], []
    more = 2 * (cap - base)
    if pooled:
        block = pl.ds(0, 2 * cap)
        across, home = at(peer((0, 1, 0), 1)), at(peer((0, 1, 0), -1))
        hops = [
            remote(send.at[block], pool, hop_send.at[0], hop_recv.at[0], across),
            remote(my_pool_ids, pool_ids, hop_send.at[1], hop_recv.at[1], across),
            remote(res.at[block], ret.at[block], hop_send.at[2], hop_recv.at[2], home),
        ]
        for j, slot in enumerate(slots[:n_near]):
            if j == own:
                continue
            cut = pl.ds(j * more, more)
            shares.append(remote(spread.at[cut], extra.at[cut], share_send.at[j], share_recv.at[j],
                                 at(peer(slot, 1))))
            parts.append(remote(extra_out.at[cut], extra_in.at[cut], part_send.at[j], part_recv.at[j],
                                at(peer(slot, -1))))

    def pack(first, last):
        spot = lax.broadcasted_iota(I32, (last - first, tokens_here), 0) + first
        pick_tok = jnp.where(spot == place_row, 1.0, 0.0).astype(BF16)
        pick_cot = jnp.where(spot == second_row, 1.0, 0.0).astype(BF16)
        pick = jnp.concatenate([pick_tok, pick_cot], axis=1)
        send[first:last] = jnp.dot(pick, stacked[...], preferred_element_type=F32).astype(BF16)

    loads[0].wait()
    loads[1].wait()
    edges = [n_near, n_near + n_far_a, count]
    groups = [(n_near, edges[1]), (0, n_near), (edges[1], count)]
    waited = False
    if pooled:
        pack(0, 2 * cap)
        pl.semaphore_wait(barrier, count - 1 + n_ctx - 1)
        waited = True
        hops[1].start()
        hops[0].start()
    for first, last in groups:
        if first == last:
            continue
        pack(off[first], off[last - 1] + size[last - 1])
        if not waited:
            pl.semaphore_wait(barrier, count - 1 + n_ctx - 1)
            waited = True
        for k in range(first, last):
            if k != own:
                fwd[k].start()

    row_e = lax.broadcasted_iota(I32, (experts, width), 0)
    router_row = jnp.sum(jnp.where(row_e == me, rw[...].astype(F32), 0.0), axis=0, keepdims=True)

    def expert_pass(x_wide, c_wide, use_term):
        m = x_wide.shape[0]
        x = x_wide.astype(BF16)
        logits = lax.dot_general(x, rw[...], NT, preferred_element_type=F32)
        lane = lax.broadcasted_iota(I32, (m, experts), 1)
        gate = jax.nn.sigmoid(jnp.sum(jnp.where(lane == me, logits, 0.0), axis=1, keepdims=True))
        upstream = (gate * c_wide).astype(BF16)
        pre = jnp.dot(x, gu[...], preferred_element_type=F32)
        a = pre[:, :hidden_units]
        u = pre[:, hidden_units:]
        s = jax.nn.sigmoid(a)
        act = a * s
        hidden = (act * u).astype(BF16)
        out = jnp.dot(hidden, dn[...], preferred_element_type=F32).astype(BF16).astype(F32)
        agreement = jnp.sum(c_wide * out, axis=1, keepdims=True)
        dense = (gate * (1.0 - gate) * agreement).astype(BF16).astype(F32)
        use_term(jnp.sum(dense * x_wide, axis=0, keepdims=True))
        moe = gate * out
        back_hidden = lax.dot_general(upstream, dn[...], NT, preferred_element_type=F32)
        back_pre = jnp.concatenate(
            [back_hidden * u * (s * (1.0 + a * (1.0 - s))), back_hidden * act], axis=1
        ).astype(BF16)
        back_in = lax.dot_general(back_pre, gu[...], NT, preferred_element_type=F32)
        grad = back_in.astype(BF16).astype(F32) + dense * router_row
        return moe, grad

    def slots_pass(first, last, use_term, with_extra=False, ready=None):
        xs, cs = [], []
        for k in range(first, last):
            if k == own:
                block = send[span(k)].astype(F32)
            else:
                fwd[k].wait_recv()
                block = recv[span(k)].astype(F32)
            xs.append(block[:size[k] // 2])
            cs.append(block[size[k] // 2:])
        if with_extra:
            for share in shares:
                share.wait_recv()
            for j in range(n_near):
                source = spread if j == own else extra
                block = source[j * more:(j + 1) * more].astype(F32)
                xs.append(block[:more // 2])
                cs.append(block[more // 2:])
        moe, grad = expert_pass(jnp.concatenate(xs, axis=0), jnp.concatenate(cs, axis=0), use_term)
        start = 0
        if with_extra:
            start = (last - first) * size[first] // 2
            for j in range(n_near):
                part = slice(start + j * more // 2, start + (j + 1) * more // 2)
                target = extra_in if j == own else extra_out
                target[j * more:(j + 1) * more] = jnp.concatenate([moe[part], grad[part]], axis=0).astype(BF16)
            for copy in parts:
                copy.start()
        each = size[first] // 2
        for i, k in enumerate(range(first, last)):
            part = slice(i * each, (i + 1) * each)
            block = jnp.concatenate([moe[part], grad[part]], axis=0).astype(BF16)
            if k == own:
                ret[span(k)] = block
            else:
                res[span(k)] = block
                if k == first and ready is not None:
                    ready()
                back[k].start()

    if pooled:
        hops[1].wait_recv()
        hops[0].wait_recv()
        wide = 2 * cap
        pr = lax.broadcasted_iota(I32, (wide, wide), 0)
        pc = lax.broadcasted_iota(I32, (wide, wide), 1)
        name_row = pool_ids[0:1, 0:wide]
        name_col = jnp.sum(jnp.where(pr == pc, jnp.broadcast_to(name_row, (wide, wide)), 0.0), axis=1, keepdims=True)
        lane, line = pc[0:1, :], pr[:, 0:1]
        mate = (name_col == name_row) & ((pr >= cap) == (pc >= cap))
        to_row = jnp.sum(jnp.where(mate & (pr < pc), 1, 0), axis=0, keepdims=True)
        to_col = jnp.sum(jnp.where(mate & (pc < pr), 1, 0), axis=1, keepdims=True)
        to_row = to_row + jnp.where(lane >= cap, more // 2, 0) + jnp.where(name_row == 0.0, AWAY, 0)
        to_col = to_col + jnp.where(line >= cap, more // 2, 0) + jnp.where(name_col == 0.0, AWAY, 0)
        for j, slot in enumerate(slots[:n_near]):
            to_dp, to_exp = peer(slot, 1)
            expert = (to_dp * n_exp + to_exp + 1).astype(F32)
            to_row = to_row + jnp.where(name_row == expert, j * more, 0)
            to_col = to_col + jnp.where(name_col == expert, j * more, 0)
        spot = lax.broadcasted_iota(I32, (n_near * more, wide), 0)
        deal = jnp.where(spot == to_row, 1.0, 0.0).astype(BF16)
        spread[...] = jnp.dot(deal, pool[...], preferred_element_type=F32).astype(BF16)
        for share in shares:
            share.start()
    loads[2].wait()
    loads[3].wait()
    router_terms = []
    tiny = []

    def scatter_column(term):
        router_sum = term
        for other in router_terms:
            router_sum = router_sum + other
        router_sum = router_sum * (1.0 / total)
        for q in range(n_ctx):
            for r in range(per):
                start = (q * per + r) * 128
                mine[q, r:r + 1, :] = router_sum[:, start:start + 128]
            if pooled:
                mine[q, per:per + 1, :] = jnp.broadcast_to(spill.astype(F32), (1, 128))
        for j in range(1, n_ctx):
            to = lax.rem(me_ctx + j, n_ctx)
            tiny.append(remote(mine.at[to], terms.at[me_ctx], ctx_send.at[j], ctx_recv.at[me_ctx], at_ctx(to)))
            tiny[-1].start()

    def send_column():
        column = mine[me_ctx]
        for j in range(1, n_ctx):
            source = lax.rem(me_ctx + j, n_ctx)
            remote(mine.at[source], terms.at[source], ctx_send.at[j], ctx_recv.at[source], at_ctx(source)).wait_recv()
            column = column + terms[source]
        summed[...] = column
        columns[me_ctx, me] = column
        for k, slot in enumerate(slots):
            if k != own:
                tiny.append(remote(summed, columns.at[me_ctx, me], col_send.at[k], col_recv.at[me], at(peer(slot, 1))))
                tiny[-1].start()

    keep, n_last = router_terms.append, (edges[1], count) if n_far_b else (0, n_near)
    if n_far_b:
        slots_pass(n_near, edges[1], keep)
        slots_pass(0, n_near, keep, pooled)
    else:
        slots_pass(n_near, edges[1], keep)
    if pooled:
        for part in parts:
            part.wait_recv()
        spot = lax.broadcasted_iota(I32, (wide, n_near * more), 1)
        gather = jnp.where(spot == to_col, 1.0, 0.0).astype(BF16)
        res[0:wide] = jnp.dot(gather, extra_in[...], preferred_element_type=F32).astype(BF16)
        hops[2].start()
    slots_pass(*n_last, scatter_column, ready=send_column)
    for k, slot in enumerate(slots):
        if k != own:
            from_dp, from_exp = peer(slot, -1)
            source = from_dp * n_exp + from_exp
            remote(summed, columns.at[me_ctx, source], col_send.at[k], col_recv.at[source],
                   at(peer(slot, -1))).wait_recv()
    for j in range(1, n_ctx):
        tiny.append(remote(columns.at[me_ctx], columns.at[me_ctx], all_send.at[j], all_recv.at[me_ctx],
                           at_ctx(lax.rem(me_ctx + j, n_ctx))))
        tiny[-1].start()

    def unpack(first, last, fresh):
        spot = lax.broadcasted_iota(I32, (tokens_here, last - first), 1) + first
        put_moe = jnp.where(spot == place_col, 1.0, 0.0).astype(BF16)
        put_grad = jnp.where(spot == second_col, 1.0, 0.0).astype(BF16)
        put = jnp.concatenate([put_moe, put_grad], axis=0)
        placed = jnp.dot(put, ret[first:last], preferred_element_type=F32)
        if fresh:
            moe_out[...] = placed[:tokens_here].astype(BF16)
            grad_out[...] = placed[tokens_here:].astype(BF16)
        else:
            moe_out[...] = (moe_out[...].astype(F32) + placed[:tokens_here]).astype(BF16)
            grad_out[...] = (grad_out[...].astype(F32) + placed[tokens_here:]).astype(BF16)

    split = edges[1] if n_far_b else count
    for k in range(split):
        if k != own:
            back[k].wait_recv()
    if pooled:
        hops[2].wait_recv()
    middle = off[split - 1] + size[split - 1]
    unpack(0, middle, True)
    if split < count:
        for k in range(split, count):
            back[k].wait_recv()
        unpack(middle, total_rows, False)

    for j in range(1, n_ctx):
        source = lax.rem(me_ctx + j, n_ctx)
        remote(columns.at[source], columns.at[source], all_send.at[j], all_recv.at[source],
               at_ctx(source)).wait_recv()
    for q in range(n_ctx):
        for r in range(per):
            start = (q * per + r) * 128
            rg_out[:, start:start + 128] = columns[q, :, r, :]
    if pooled:
        flag_out[0, 0] = jnp.max(columns[0, :, per, :])
    else:
        flag_out[0, 0] = jnp.float32(0.0)
    for copy in fwd + back + hops + shares + parts:
        if copy is not None:
            copy.wait_send()
    for copy in tiny:
        copy.wait_send()


def hand_over(moe, grad, columns, moe_out, grad_out, rg_out, moe_buf, grad_buf, rg_buf, in_sem, out_sem):
    half = moe.shape[0] // 2
    parts = [(columns, rg_buf, rg_out)]
    for source, buffer, target in ((moe, moe_buf, moe_out), (grad, grad_buf, grad_out)):
        for start in (0, half):
            cut = pl.ds(start, half)
            parts.append((source.at[cut], buffer.at[cut], target.at[cut]))
    loads, stores = [], []
    for i, (source, buffer, target) in enumerate(parts):
        loads.append(pltpu.make_async_copy(source, buffer, in_sem.at[i]))
        stores.append(pltpu.make_async_copy(buffer, target, out_sem.at[i]))
    for load in loads:
        load.start()
    for load, store in zip(loads, stores):
        load.wait()
        store.start()
    for store in stores:
        store.wait()


def send_out(moe, grad, columns, moe_out, grad_out, rg_out, sem):
    half = moe.shape[0] // 2
    copies = [(columns, rg_out)]
    for source, target in ((moe, moe_out), (grad, grad_out)):
        for start in (0, half):
            cut = pl.ds(start, half)
            copies.append((source.at[cut], target.at[cut]))
    copies = [pltpu.make_async_copy(a, b, sem.at[i]) for i, (a, b) in enumerate(copies)]
    for copy in copies:
        copy.start()
    for copy in copies:
        copy.wait()


def exchange(shape, base, collective, tokens, cotangent, ids, router, gate_up, down_weight):
    n_dp, n_ctx, n_exp = shape
    tok_count, width = tokens.shape
    experts = router.shape[0]
    hidden_units = down_weight.shape[1]
    cap = capacity(tok_count, experts)
    slots, counts, _, _, total_rows, pooled = layout(n_dp, n_exp, cap, base)
    count, n_near = len(slots), counts[0]
    total = tok_count * n_dp * n_ctx * n_exp
    piece = -(-(width // 128 // n_ctx + 1) // 8) * 8
    vmem = pl.BlockSpec(memory_space=pltpu.VMEM)
    hbm = pl.BlockSpec(memory_space=pl.ANY)
    dma = pltpu.SemaphoreType.DMA
    rows = pltpu.VMEM((total_rows, width), BF16)
    more = pltpu.VMEM((n_near * 2 * (cap - base), width), BF16)
    names = pltpu.VMEM((8, 128), F32)
    scratch = [
        pltpu.VMEM((2 * tok_count, width), BF16),
        rows, rows, rows, rows,
        pltpu.VMEM((width, 2 * hidden_units), BF16),
        pltpu.VMEM((hidden_units, width), BF16),
        pltpu.VMEM((n_ctx, piece, 128), F32),
        pltpu.VMEM((piece, 128), F32),
        pltpu.VMEM((n_ctx, piece, 128), F32),
        pltpu.VMEM((n_ctx, experts, piece, 128), F32),
        dma((4,)),
        dma((count,)), dma((count,)), dma((count,)), dma((count,)),
        dma((n_ctx,)), dma((n_ctx,)),
        dma((count,)), dma((count,)),
        dma((n_ctx,)), dma((n_ctx,)),
    ]
    if pooled:
        scratch += [
            pltpu.VMEM((2 * cap, width), BF16), names, names, more, more, more, more,
            dma((3,)), dma((3,)), dma((n_near,)), dma((n_near,)), dma((n_near,)), dma((n_near,)),
        ]
    flops = 2 * 2 * count * cap * width * 3 * hidden_units
    return pl.pallas_call(
        functools.partial(kernel, n_dp, n_ctx, n_exp, cap, base, total),
        out_shape=(
            jax.ShapeDtypeStruct((tok_count, width), BF16),
            jax.ShapeDtypeStruct((tok_count, width), BF16),
            jax.ShapeDtypeStruct((experts, width), F32),
            jax.ShapeDtypeStruct((1, 1), F32),
        ),
        in_specs=[hbm, hbm, vmem, vmem, hbm, hbm],
        out_specs=(vmem, vmem, vmem, pl.BlockSpec(memory_space=pltpu.SMEM)),
        scratch_shapes=scratch,
        compiler_params=pltpu.CompilerParams(
            collective_id=collective, has_side_effects=True, vmem_limit_bytes=58 * 1024 * 1024
        ),
        cost_estimate=pl.CostEstimate(
            flops=flops, bytes_accessed=12 * 1024 * 1024, transcendentals=0
        ),
    )(tokens, cotangent, ids, router, gate_up, down_weight)


def deliver_now(moe, grad, columns):
    hbm = pl.BlockSpec(memory_space=pl.ANY)
    return pl.pallas_call(
        send_out,
        out_shape=tuple(jax.ShapeDtypeStruct(v.shape, v.dtype) for v in (moe, grad, columns)),
        in_specs=[hbm, hbm, hbm],
        out_specs=(hbm, hbm, hbm),
        scratch_shapes=[pltpu.SemaphoreType.DMA((5,))],
    )(moe, grad, columns)


def deliver(moe, grad, columns):
    hbm = pl.BlockSpec(memory_space=pl.ANY)
    dma = pltpu.SemaphoreType.DMA
    return pl.pallas_call(
        hand_over,
        out_shape=tuple(jax.ShapeDtypeStruct(v.shape, v.dtype) for v in (moe, grad, columns)),
        in_specs=[hbm, hbm, hbm],
        out_specs=(hbm, hbm, hbm),
        scratch_shapes=[
            pltpu.VMEM(moe.shape, BF16),
            pltpu.VMEM(grad.shape, BF16),
            pltpu.VMEM(columns.shape, F32),
            dma((5,)),
            dma((5,)),
        ],
    )(moe, grad, columns)


def capacity(tok_count, experts):
    most = min(tok_count, 3 * tok_count // (2 * experts))
    return -(-most // 8) * 8


def per_device(n_dp, n_ctx, n_exp, tokens, cotangent, expert_ids, router_weight, gate_up, down_weight):
    tok_count = tokens.shape[0]
    cap = capacity(tok_count, router_weight.shape[1])
    base = min(cap, -(-(2 * cap // 3) // 8) * 8)
    shape = (n_dp, n_ctx, n_exp)
    args = (tokens, cotangent, expert_ids.reshape(1, tok_count), router_weight.T, gate_up, down_weight)
    moe, grad, columns, spilled = exchange(shape, base, 0, *args)
    if base == cap:
        moe, grad, columns = deliver(moe, grad, columns)
        return moe, grad, columns.T

    def short(moe, grad, columns, *args):
        return deliver_now(moe, grad, columns)

    def full(moe, grad, columns, *args):
        return deliver(*exchange(shape, cap, 1, *args)[:3])

    moe, grad, columns = lax.cond(spilled[0, 0] > 0.0, full, short, moe, grad, columns, *args)
    return moe, grad, columns.T


def solution(mesh):
    in_specs = (
        P(("dp", "ctx", "exp"), None),
        P(("dp", "ctx", "exp"), None),
        P(("dp", "ctx", "exp"), None),
        P(),
        P(("dp", "exp"), None, None),
        P(("dp", "exp"), None, None),
    )
    out_specs = (P(("dp", "ctx", "exp"), None), P(("dp", "ctx", "exp"), None), P())
    shape = mesh.shape
    return jax.shard_map(
        functools.partial(per_device, shape["dp"], shape["ctx"], shape["exp"]),
        mesh=mesh, in_specs=in_specs, out_specs=out_specs, check_vma=False,
    )
```

```python
import functools

import jax
import jax.numpy as jnp
from jax import lax
from jax.experimental import pallas as pl
from jax.experimental.pallas import tpu as pltpu
from jax.sharding import PartitionSpec as P

MESH = pl.DeviceIdType.MESH
F32 = jnp.float32
BF16 = jnp.bfloat16
I32 = jnp.int32
NT = (((1,), (1,)), ((), ()))
AWAY = -(1 << 20)


def plan(n_dp, n_exp):
    half = n_exp // 2
    cut = (half + 1) // 2
    near = [(d, 0, o) for o in range(half) for d in range(n_dp)]
    far = [(d, 1, o) for d in range(n_dp) for o in range(half)]
    far_a, far_b = far[:n_dp * cut], far[n_dp * cut:]
    return near, far_a, far_b


def layout(n_dp, n_exp, cap, base):
    near, far_a, far_b = plan(n_dp, n_exp)
    slots = near + far_a + far_b
    pooled = base < cap
    offsets, sizes, at = [], [], 2 * cap if pooled else 0
    for _, h, _ in slots:
        offsets.append(at)
        sizes.append(2 * (base if h else cap))
        at += sizes[-1]
    return slots, (len(near), len(far_a), len(far_b)), offsets, sizes, at, pooled


def kernel(n_dp, n_ctx, n_exp, cap, base, total, *refs):
    (tok_hbm, cot_hbm, ids, rw, gu_hbm, dn_hbm, moe_out, grad_out, rg_out, flag_out,
     stacked, send, recv, res, ret, gu, dn, mine, summed, terms, columns,
     w_sem, fwd_send, fwd_recv, ret_send, ret_recv,
     ctx_send, ctx_recv, col_send, col_recv, all_send, all_recv) = refs[:32]
    slots, (n_near, n_far_a, n_far_b), off, size, total_rows, pooled = layout(n_dp, n_exp, cap, base)
    if pooled:
        (pool, pool_ids, my_pool_ids, spread, extra, extra_out, extra_in,
         hop_send, hop_recv, share_send, share_recv, part_send, part_recv) = refs[32:]
    me_dp, me_ctx, me_exp = lax.axis_index("dp"), lax.axis_index("ctx"), lax.axis_index("exp")
    me = me_dp * n_exp + me_exp
    half = n_exp // 2
    count = len(slots)
    own = slots.index((0, 0, 0))
    tokens_here = stacked.shape[0] // 2
    width = stacked.shape[1]
    hidden_units = dn.shape[0]
    experts = rw.shape[0]
    per = width // 128 // n_ctx

    def peer(slot, way):
        d, h, o = slot
        if way < 0:
            d, h, o = (n_dp - d) % n_dp, h, (half - o) % half
        to_dp = lax.rem(me_dp + d, n_dp)
        to_half = lax.rem(me_exp // half + h, 2)
        to_low = lax.rem(lax.rem(me_exp, half) + o, half)
        return to_dp, to_half * half + to_low

    def at(pair):
        return {"dp": pair[0], "ctx": me_ctx, "exp": pair[1]}

    def at_ctx(j):
        return {"dp": me_dp, "ctx": j, "exp": me_exp}

    def remote(source, target, sent, came, where):
        return pltpu.make_async_remote_copy(
            src_ref=source, dst_ref=target, send_sem=sent, recv_sem=came,
            device_id=where, device_id_type=MESH,
        )

    def span(k):
        return pl.ds(off[k], size[k])

    barrier = pltpu.get_barrier_semaphore()
    for k, slot in enumerate(slots):
        if k != own:
            pl.semaphore_signal(barrier, inc=1, device_id=at(peer(slot, 1)), device_id_type=MESH)
    for j in range(1, n_ctx):
        pl.semaphore_signal(
            barrier, inc=1, device_id=at_ctx(lax.rem(me_ctx + j, n_ctx)), device_id_type=MESH
        )
    loads = [
        pltpu.make_async_copy(tok_hbm, stacked.at[pl.ds(0, tokens_here)], w_sem.at[0]),
        pltpu.make_async_copy(cot_hbm, stacked.at[pl.ds(tokens_here, tokens_here)], w_sem.at[1]),
        pltpu.make_async_copy(gu_hbm.at[0], gu, w_sem.at[2]),
        pltpu.make_async_copy(dn_hbm.at[0], dn, w_sem.at[3]),
    ]
    for load in loads:
        load.start()

    ids_row = ids[...]
    r_iota = lax.broadcasted_iota(I32, (tokens_here, tokens_here), 0)
    c_iota = lax.broadcasted_iota(I32, (tokens_here, tokens_here), 1)
    ids_wide = jnp.broadcast_to(ids_row, (tokens_here, tokens_here))
    ids_col = jnp.sum(jnp.where(r_iota == c_iota, ids_wide, 0), axis=1, keepdims=True)
    same = ids_col == ids_row
    rank_row = jnp.sum(jnp.where(same & (r_iota < c_iota), 1, 0), axis=0, keepdims=True)
    rank_col = jnp.sum(jnp.where(same & (c_iota < r_iota), 1, 0), axis=1, keepdims=True)
    place_row, place_col = rank_row, rank_col
    far_row, far_col = jnp.zeros_like(ids_row), jnp.zeros_like(ids_col)
    for k, slot in enumerate(slots):
        to_dp, to_exp = peer(slot, 1)
        expert = to_dp * n_exp + to_exp
        place_row = place_row + jnp.where(ids_row == expert, off[k], 0)
        place_col = place_col + jnp.where(ids_col == expert, off[k], 0)
        if slot[1] and pooled:
            far_row = far_row + jnp.where(ids_row == expert, 1, 0)
            far_col = far_col + jnp.where(ids_col == expert, 1, 0)
    second_row, second_col = place_row + cap, place_col + cap
    if pooled:
        over_row = jnp.where(rank_row >= base, far_row, 0)
        over_col = jnp.where(rank_col >= base, far_col, 0)
        turn_row = jnp.sum(jnp.where(r_iota < c_iota, over_col, 0), axis=0, keepdims=True)
        turn_col = jnp.sum(jnp.where(c_iota < r_iota, over_row, 0), axis=1, keepdims=True)
        spill = jnp.sum(jnp.where(turn_row >= cap, over_row, 0), axis=1, keepdims=True)
        turn_row = jnp.where(turn_row >= cap, AWAY, turn_row)
        turn_col = jnp.where(turn_col >= cap, AWAY, turn_col)
        second_row = jnp.where(over_row == 1, turn_row + cap, place_row + jnp.where(far_row == 1, base, cap))
        second_col = jnp.where(over_col == 1, turn_col + cap, place_col + jnp.where(far_col == 1, base, cap))
        place_row = jnp.where(over_row == 1, turn_row, place_row)
        place_col = jnp.where(over_col == 1, turn_col, place_col)
        here = (turn_col == c_iota) | (turn_col + cap == c_iota)
        named = jnp.where((over_col == 1) & here, ids_col + 1, 0)
        my_pool_ids[...] = jnp.broadcast_to(
            jnp.sum(named, axis=0, keepdims=True).astype(F32), my_pool_ids.shape
        )

    fwd, back = [], []
    for k, slot in enumerate(slots):
        if k == own:
            fwd.append(None)
            back.append(None)
            continue
        fwd.append(remote(send.at[span(k)], recv.at[span(k)], fwd_send.at[k], fwd_recv.at[k],
                          at(peer(slot, 1))))
        back.append(remote(res.at[span(k)], ret.at[span(k)], ret_send.at[k], ret_recv.at[k],
                           at(peer(slot, -1))))
    hops, shares, parts = [], [], []
    more = 2 * (cap - base)
    if pooled:
        block = pl.ds(0, 2 * cap)
        across, home = at(peer((0, 1, 0), 1)), at(peer((0, 1, 0), -1))
        hops = [
            remote(send.at[block], pool, hop_send.at[0], hop_recv.at[0], across),
            remote(my_pool_ids, pool_ids, hop_send.at[1], hop_recv.at[1], across),
            remote(res.at[block], ret.at[block], hop_send.at[2], hop_recv.at[2], home),
        ]
        for j, slot in enumerate(slots[:n_near]):
            if j == own:
                continue
            cut = pl.ds(j * more, more)
            shares.append(remote(spread.at[cut], extra.at[cut], share_send.at[j], share_recv.at[j],
                                 at(peer(slot, 1))))
            parts.append(remote(extra_out.at[cut], extra_in.at[cut], part_send.at[j], part_recv.at[j],
                                at(peer(slot, -1))))

    def pack(first, last):
        spot = lax.broadcasted_iota(I32, (last - first, tokens_here), 0) + first
        pick_tok = jnp.where(spot == place_row, 1.0, 0.0).astype(BF16)
        pick_cot = jnp.where(spot == second_row, 1.0, 0.0).astype(BF16)
        pick = jnp.concatenate([pick_tok, pick_cot], axis=1)
        send[first:last] = jnp.dot(pick, stacked[...], preferred_element_type=F32).astype(BF16)

    loads[0].wait()
    loads[1].wait()
    edges = [n_near, n_near + n_far_a, count]
    groups = [(n_near, edges[1]), (0, n_near), (edges[1], count)]
    waited = False
    if pooled:
        pack(0, 2 * cap)
        pl.semaphore_wait(barrier, count - 1 + n_ctx - 1)
        waited = True
        hops[1].start()
        hops[0].start()
    for first, last in groups:
        if first == last:
            continue
        pack(off[first], off[last - 1] + size[last - 1])
        if not waited:
            pl.semaphore_wait(barrier, count - 1 + n_ctx - 1)
            waited = True
        for k in range(first, last):
            if k != own:
                fwd[k].start()

    row_e = lax.broadcasted_iota(I32, (experts, width), 0)
    router_row = jnp.sum(jnp.where(row_e == me, rw[...].astype(F32), 0.0), axis=0, keepdims=True)

    def expert_pass(x_wide, c_wide, use_term):
        m = x_wide.shape[0]
        x = x_wide.astype(BF16)
        logits = lax.dot_general(x, rw[...], NT, preferred_element_type=F32)
        lane = lax.broadcasted_iota(I32, (m, experts), 1)
        gate = jax.nn.sigmoid(jnp.sum(jnp.where(lane == me, logits, 0.0), axis=1, keepdims=True))
        upstream = (gate * c_wide).astype(BF16)
        pre = jnp.dot(x, gu[...], preferred_element_type=F32)
        a = pre[:, :hidden_units]
        u = pre[:, hidden_units:]
        s = jax.nn.sigmoid(a)
        act = a * s
        hidden = (act * u).astype(BF16)
        out = jnp.dot(hidden, dn[...], preferred_element_type=F32).astype(BF16).astype(F32)
        agreement = jnp.sum(c_wide * out, axis=1, keepdims=True)
        dense = (gate * (1.0 - gate) * agreement).astype(BF16).astype(F32)
        use_term(jnp.sum(dense * x_wide, axis=0, keepdims=True))
        moe = gate * out
        back_hidden = lax.dot_general(upstream, dn[...], NT, preferred_element_type=F32)
        back_pre = jnp.concatenate(
            [back_hidden * u * (s * (1.0 + a * (1.0 - s))), back_hidden * act], axis=1
        ).astype(BF16)
        back_in = lax.dot_general(back_pre, gu[...], NT, preferred_element_type=F32)
        grad = back_in.astype(BF16).astype(F32) + dense * router_row
        return moe, grad

    def slots_pass(first, last, use_term, with_extra=False, ready=None):
        xs, cs = [], []
        for k in range(first, last):
            if k == own:
                block = send[span(k)].astype(F32)
            else:
                fwd[k].wait_recv()
                block = recv[span(k)].astype(F32)
            xs.append(block[:size[k] // 2])
            cs.append(block[size[k] // 2:])
        if with_extra:
            for share in shares:
                share.wait_recv()
            for j in range(n_near):
                source = spread if j == own else extra
                block = source[j * more:(j + 1) * more].astype(F32)
                xs.append(block[:more // 2])
                cs.append(block[more // 2:])
        moe, grad = expert_pass(jnp.concatenate(xs, axis=0), jnp.concatenate(cs, axis=0), use_term)
        start = 0
        if with_extra:
            start = (last - first) * size[first] // 2
            for j in range(n_near):
                part = slice(start + j * more // 2, start + (j + 1) * more // 2)
                target = extra_in if j == own else extra_out
                target[j * more:(j + 1) * more] = jnp.concatenate([moe[part], grad[part]], axis=0).astype(BF16)
            for copy in parts:
                copy.start()
        each = size[first] // 2
        for i, k in enumerate(range(first, last)):
            part = slice(i * each, (i + 1) * each)
            block = jnp.concatenate([moe[part], grad[part]], axis=0).astype(BF16)
            if k == own:
                ret[span(k)] = block
            else:
                res[span(k)] = block
                if k == first and ready is not None:
                    ready()
                back[k].start()

    if pooled:
        hops[1].wait_recv()
        hops[0].wait_recv()
        wide = 2 * cap
        pr = lax.broadcasted_iota(I32, (wide, wide), 0)
        pc = lax.broadcasted_iota(I32, (wide, wide), 1)
        name_row = pool_ids[0:1, 0:wide]
        name_col = jnp.sum(jnp.where(pr == pc, jnp.broadcast_to(name_row, (wide, wide)), 0.0), axis=1, keepdims=True)
        lane, line = pc[0:1, :], pr[:, 0:1]
        mate = (name_col == name_row) & ((pr >= cap) == (pc >= cap))
        to_row = jnp.sum(jnp.where(mate & (pr < pc), 1, 0), axis=0, keepdims=True)
        to_col = jnp.sum(jnp.where(mate & (pc < pr), 1, 0), axis=1, keepdims=True)
        to_row = to_row + jnp.where(lane >= cap, more // 2, 0) + jnp.where(name_row == 0.0, AWAY, 0)
        to_col = to_col + jnp.where(line >= cap, more // 2, 0) + jnp.where(name_col == 0.0, AWAY, 0)
        for j, slot in enumerate(slots[:n_near]):
            to_dp, to_exp = peer(slot, 1)
            expert = (to_dp * n_exp + to_exp + 1).astype(F32)
            to_row = to_row + jnp.where(name_row == expert, j * more, 0)
            to_col = to_col + jnp.where(name_col == expert, j * more, 0)
        spot = lax.broadcasted_iota(I32, (n_near * more, wide), 0)
        deal = jnp.where(spot == to_row, 1.0, 0.0).astype(BF16)
        spread[...] = jnp.dot(deal, pool[...], preferred_element_type=F32).astype(BF16)
        for share in shares:
            share.start()
    loads[2].wait()
    loads[3].wait()
    router_terms = []
    tiny = []

    def scatter_column(term):
        router_sum = term
        for other in router_terms:
            router_sum = router_sum + other
        router_sum = router_sum * (1.0 / total)
        for q in range(n_ctx):
            for r in range(per):
                start = (q * per + r) * 128
                mine[q, r:r + 1, :] = router_sum[:, start:start + 128]
            if pooled:
                mine[q, per:per + 1, :] = jnp.broadcast_to(spill.astype(F32), (1, 128))
        for j in range(1, n_ctx):
            to = lax.rem(me_ctx + j, n_ctx)
            tiny.append(remote(mine.at[to], terms.at[me_ctx], ctx_send.at[j], ctx_recv.at[me_ctx], at_ctx(to)))
            tiny[-1].start()

    def send_column():
        column = mine[me_ctx]
        for j in range(1, n_ctx):
            source = lax.rem(me_ctx + j, n_ctx)
            remote(mine.at[source], terms.at[source], ctx_send.at[j], ctx_recv.at[source], at_ctx(source)).wait_recv()
            column = column + terms[source]
        summed[...] = column
        columns[me_ctx, me] = column
        for k, slot in enumerate(slots):
            if k != own:
                tiny.append(remote(summed, columns.at[me_ctx, me], col_send.at[k], col_recv.at[me], at(peer(slot, 1))))
                tiny[-1].start()

    keep, n_last = router_terms.append, (edges[1], count) if n_far_b else (0, n_near)
    if n_far_b:
        slots_pass(n_near, edges[1], keep)
        slots_pass(0, n_near, keep, pooled)
    else:
        slots_pass(n_near, edges[1], keep)
    if pooled:
        for part in parts:
            part.wait_recv()
        spot = lax.broadcasted_iota(I32, (wide, n_near * more), 1)
        gather = jnp.where(spot == to_col, 1.0, 0.0).astype(BF16)
        res[0:wide] = jnp.dot(gather, extra_in[...], preferred_element_type=F32).astype(BF16)
        hops[2].start()
    slots_pass(*n_last, scatter_column, ready=send_column)
    for k, slot in enumerate(slots):
        if k != own:
            from_dp, from_exp = peer(slot, -1)
            source = from_dp * n_exp + from_exp
            remote(summed, columns.at[me_ctx, source], col_send.at[k], col_recv.at[source],
                   at(peer(slot, -1))).wait_recv()
    for j in range(1, n_ctx):
        tiny.append(remote(columns.at[me_ctx], columns.at[me_ctx], all_send.at[j], all_recv.at[me_ctx],
                           at_ctx(lax.rem(me_ctx + j, n_ctx))))
        tiny[-1].start()

    def unpack(first, last, fresh):
        spot = lax.broadcasted_iota(I32, (tokens_here, last - first), 1) + first
        put_moe = jnp.where(spot == place_col, 1.0, 0.0).astype(BF16)
        put_grad = jnp.where(spot == second_col, 1.0, 0.0).astype(BF16)
        put = jnp.concatenate([put_moe, put_grad], axis=0)
        placed = jnp.dot(put, ret[first:last], preferred_element_type=F32)
        if fresh:
            moe_out[...] = placed[:tokens_here].astype(BF16)
            grad_out[...] = placed[tokens_here:].astype(BF16)
        else:
            moe_out[...] = (moe_out[...].astype(F32) + placed[:tokens_here]).astype(BF16)
            grad_out[...] = (grad_out[...].astype(F32) + placed[tokens_here:]).astype(BF16)

    split = edges[1] if n_far_b else count
    for k in range(split):
        if k != own:
            back[k].wait_recv()
    if pooled:
        hops[2].wait_recv()
    middle = off[split - 1] + size[split - 1]
    unpack(0, middle, True)
    if split < count:
        for k in range(split, count):
            back[k].wait_recv()
        unpack(middle, total_rows, False)

    for j in range(1, n_ctx):
        source = lax.rem(me_ctx + j, n_ctx)
        remote(columns.at[source], columns.at[source], all_send.at[j], all_recv.at[source],
               at_ctx(source)).wait_recv()
    for q in range(n_ctx):
        for r in range(per):
            start = (q * per + r) * 128
            rg_out[:, start:start + 128] = columns[q, :, r, :]
    if pooled:
        flag_out[0, 0] = jnp.where(jnp.max(columns[0, :, per, :]) > 0.0, 1, 0)
    else:
        flag_out[0, 0] = jnp.int32(0)
    for copy in fwd + back + hops + shares + parts:
        if copy is not None:
            copy.wait_send()
    for copy in tiny:
        copy.wait_send()


def hand_over(moe, grad, columns, moe_out, grad_out, rg_out, moe_buf, grad_buf, rg_buf, in_sem, out_sem):
    half = moe.shape[0] // 2
    parts = [(columns, rg_buf, rg_out)]
    for source, buffer, target in ((moe, moe_buf, moe_out), (grad, grad_buf, grad_out)):
        for start in (0, half):
            cut = pl.ds(start, half)
            parts.append((source.at[cut], buffer.at[cut], target.at[cut]))
    loads, stores = [], []
    for i, (source, buffer, target) in enumerate(parts):
        loads.append(pltpu.make_async_copy(source, buffer, in_sem.at[i]))
        stores.append(pltpu.make_async_copy(buffer, target, out_sem.at[i]))
    for load in loads:
        load.start()
    for load, store in zip(loads, stores):
        load.wait()
        store.start()
    for store in stores:
        store.wait()


def send_out(moe, grad, columns, moe_out, grad_out, rg_out, sem):
    half = moe.shape[0] // 2
    copies = [(columns, rg_out)]
    for source, target in ((moe, moe_out), (grad, grad_out)):
        for start in (0, half):
            cut = pl.ds(start, half)
            copies.append((source.at[cut], target.at[cut]))
    copies = [pltpu.make_async_copy(a, b, sem.at[i]) for i, (a, b) in enumerate(copies)]
    for copy in copies:
        copy.start()
    for copy in copies:
        copy.wait()


def exchange(shape, base, collective, tokens, cotangent, ids, router, gate_up, down_weight):
    n_dp, n_ctx, n_exp = shape
    tok_count, width = tokens.shape
    experts = router.shape[0]
    hidden_units = down_weight.shape[1]
    cap = capacity(tok_count, experts)
    slots, counts, _, _, total_rows, pooled = layout(n_dp, n_exp, cap, base)
    count, n_near = len(slots), counts[0]
    total = tok_count * n_dp * n_ctx * n_exp
    piece = -(-(width // 128 // n_ctx + 1) // 8) * 8
    vmem = pl.BlockSpec(memory_space=pltpu.VMEM)
    hbm = pl.BlockSpec(memory_space=pl.ANY)
    dma = pltpu.SemaphoreType.DMA
    rows = pltpu.VMEM((total_rows, width), BF16)
    more = pltpu.VMEM((n_near * 2 * (cap - base), width), BF16)
    names = pltpu.VMEM((8, 128), F32)
    scratch = [
        pltpu.VMEM((2 * tok_count, width), BF16),
        rows, rows, rows, rows,
        pltpu.VMEM((width, 2 * hidden_units), BF16),
        pltpu.VMEM((hidden_units, width), BF16),
        pltpu.VMEM((n_ctx, piece, 128), F32),
        pltpu.VMEM((piece, 128), F32),
        pltpu.VMEM((n_ctx, piece, 128), F32),
        pltpu.VMEM((n_ctx, experts, piece, 128), F32),
        dma((4,)),
        dma((count,)), dma((count,)), dma((count,)), dma((count,)),
        dma((n_ctx,)), dma((n_ctx,)),
        dma((count,)), dma((count,)),
        dma((n_ctx,)), dma((n_ctx,)),
    ]
    if pooled:
        scratch += [
            pltpu.VMEM((2 * cap, width), BF16), names, names, more, more, more, more,
            dma((3,)), dma((3,)), dma((n_near,)), dma((n_near,)), dma((n_near,)), dma((n_near,)),
        ]
    flops = 2 * 2 * count * cap * width * 3 * hidden_units
    return pl.pallas_call(
        functools.partial(kernel, n_dp, n_ctx, n_exp, cap, base, total),
        out_shape=(
            jax.ShapeDtypeStruct((tok_count, width), BF16),
            jax.ShapeDtypeStruct((tok_count, width), BF16),
            jax.ShapeDtypeStruct((experts, width), F32),
            jax.ShapeDtypeStruct((1, 1), I32),
        ),
        in_specs=[hbm, hbm, vmem, vmem, hbm, hbm],
        out_specs=(vmem, vmem, vmem, pl.BlockSpec(memory_space=pltpu.SMEM)),
        scratch_shapes=scratch,
        compiler_params=pltpu.CompilerParams(
            collective_id=collective, has_side_effects=True, vmem_limit_bytes=58 * 1024 * 1024
        ),
        cost_estimate=pl.CostEstimate(
            flops=flops, bytes_accessed=12 * 1024 * 1024, transcendentals=0
        ),
    )(tokens, cotangent, ids, router, gate_up, down_weight)


def deliver_now(moe, grad, columns):
    hbm = pl.BlockSpec(memory_space=pl.ANY)
    return pl.pallas_call(
        send_out,
        out_shape=tuple(jax.ShapeDtypeStruct(v.shape, v.dtype) for v in (moe, grad, columns)),
        in_specs=[hbm, hbm, hbm],
        out_specs=(hbm, hbm, hbm),
        scratch_shapes=[pltpu.SemaphoreType.DMA((5,))],
    )(moe, grad, columns)


def deliver(moe, grad, columns):
    hbm = pl.BlockSpec(memory_space=pl.ANY)
    dma = pltpu.SemaphoreType.DMA
    return pl.pallas_call(
        hand_over,
        out_shape=tuple(jax.ShapeDtypeStruct(v.shape, v.dtype) for v in (moe, grad, columns)),
        in_specs=[hbm, hbm, hbm],
        out_specs=(hbm, hbm, hbm),
        scratch_shapes=[
            pltpu.VMEM(moe.shape, BF16),
            pltpu.VMEM(grad.shape, BF16),
            pltpu.VMEM(columns.shape, F32),
            dma((5,)),
            dma((5,)),
        ],
    )(moe, grad, columns)


def capacity(tok_count, experts):
    most = min(tok_count, 3 * tok_count // (2 * experts))
    return -(-most // 8) * 8


def per_device(n_dp, n_ctx, n_exp, tokens, cotangent, expert_ids, router_weight, gate_up, down_weight):
    tok_count = tokens.shape[0]
    cap = capacity(tok_count, router_weight.shape[1])
    base = min(cap, -(-(2 * cap // 3) // 8) * 8)
    shape = (n_dp, n_ctx, n_exp)
    args = (tokens, cotangent, expert_ids.reshape(1, tok_count), router_weight.T, gate_up, down_weight)
    moe, grad, columns, spilled = exchange(shape, base, 0, *args)
    if base == cap:
        moe, grad, columns = deliver(moe, grad, columns)
        return moe, grad, columns.T

    def short(moe, grad, columns, *args):
        return deliver_now(moe, grad, columns)

    def full(moe, grad, columns, *args):
        return deliver(*exchange(shape, cap, 1, *args)[:3])

    moe, grad, columns = lax.switch(spilled[0, 0], (short, full), moe, grad, columns, *args)
    return moe, grad, columns.T


def solution(mesh):
    in_specs = (
        P(("dp", "ctx", "exp"), None),
        P(("dp", "ctx", "exp"), None),
        P(("dp", "ctx", "exp"), None),
        P(),
        P(("dp", "exp"), None, None),
        P(("dp", "exp"), None, None),
    )
    out_specs = (P(("dp", "ctx", "exp"), None), P(("dp", "ctx", "exp"), None), P())
    shape = mesh.shape
    return jax.shard_map(
        functools.partial(per_device, shape["dp"], shape["ctx"], shape["exp"]),
        mesh=mesh, in_specs=in_specs, out_specs=out_specs, check_vma=False,
    )
```

```python
import functools

import jax
import jax.numpy as jnp
from jax import lax
from jax.experimental import pallas as pl
from jax.experimental.pallas import tpu as pltpu
from jax.sharding import PartitionSpec as P

MESH = pl.DeviceIdType.MESH
F32 = jnp.float32
BF16 = jnp.bfloat16
I32 = jnp.int32
NT = (((1,), (1,)), ((), ()))
AWAY = -(1 << 20)


def plan(n_dp, n_exp):
    half = n_exp // 2
    cut = (half + 1) // 2
    near = [(d, 0, o) for o in range(half) for d in range(n_dp)]
    far = [(d, 1, o) for d in range(n_dp) for o in range(half)]
    far_a, far_b = far[:n_dp * cut], far[n_dp * cut:]
    return near, far_a, far_b


def layout(n_dp, n_exp, cap, base):
    near, far_a, far_b = plan(n_dp, n_exp)
    slots = near + far_a + far_b
    pooled = base < cap
    offsets, sizes, at = [], [], 2 * cap if pooled else 0
    for _, h, _ in slots:
        offsets.append(at)
        sizes.append(2 * (base if h else cap))
        at += sizes[-1]
    return slots, (len(near), len(far_a), len(far_b)), offsets, sizes, at, pooled


def kernel(n_dp, n_ctx, n_exp, cap, base, total, *refs):
    (tok_hbm, cot_hbm, ids, rw, gu_hbm, dn_hbm, moe_out, grad_out, rg_out, flag_out,
     stacked, send, recv, res, ret, gu, dn, mine, summed, terms, columns,
     w_sem, fwd_send, fwd_recv, ret_send, ret_recv,
     ctx_send, ctx_recv, col_send, col_recv, all_send, all_recv) = refs[:32]
    slots, (n_near, n_far_a, n_far_b), off, size, total_rows, pooled = layout(n_dp, n_exp, cap, base)
    if pooled:
        (pool, pool_ids, my_pool_ids, spread, extra, extra_out, extra_in,
         hop_send, hop_recv, share_send, share_recv, part_send, part_recv) = refs[32:]
    me_dp, me_ctx, me_exp = lax.axis_index("dp"), lax.axis_index("ctx"), lax.axis_index("exp")
    me = me_dp * n_exp + me_exp
    half = n_exp // 2
    count = len(slots)
    own = slots.index((0, 0, 0))
    tokens_here = stacked.shape[0] // 2
    width = stacked.shape[1]
    hidden_units = dn.shape[0]
    experts = rw.shape[0]
    per = width // 128 // n_ctx

    def peer(slot, way):
        d, h, o = slot
        if way < 0:
            d, h, o = (n_dp - d) % n_dp, h, (half - o) % half
        to_dp = lax.rem(me_dp + d, n_dp)
        to_half = lax.rem(me_exp // half + h, 2)
        to_low = lax.rem(lax.rem(me_exp, half) + o, half)
        return to_dp, to_half * half + to_low

    def at(pair):
        return {"dp": pair[0], "ctx": me_ctx, "exp": pair[1]}

    def at_ctx(j):
        return {"dp": me_dp, "ctx": j, "exp": me_exp}

    def remote(source, target, sent, came, where):
        return pltpu.make_async_remote_copy(
            src_ref=source, dst_ref=target, send_sem=sent, recv_sem=came,
            device_id=where, device_id_type=MESH,
        )

    def span(k):
        return pl.ds(off[k], size[k])

    barrier = pltpu.get_barrier_semaphore()
    for k, slot in list(enumerate(slots))[::-1]:
        if k != own:
            pl.semaphore_signal(barrier, inc=1, device_id=at(peer(slot, 1)), device_id_type=MESH)
    for j in range(1, n_ctx):
        pl.semaphore_signal(
            barrier, inc=1, device_id=at_ctx(lax.rem(me_ctx + j, n_ctx)), device_id_type=MESH
        )
    loads = [
        pltpu.make_async_copy(tok_hbm, stacked.at[pl.ds(0, tokens_here)], w_sem.at[0]),
        pltpu.make_async_copy(cot_hbm, stacked.at[pl.ds(tokens_here, tokens_here)], w_sem.at[1]),
        pltpu.make_async_copy(gu_hbm.at[0], gu, w_sem.at[2]),
        pltpu.make_async_copy(dn_hbm.at[0], dn, w_sem.at[3]),
    ]
    for load in loads:
        load.start()

    ids_row = ids[...]
    r_iota = lax.broadcasted_iota(I32, (tokens_here, tokens_here), 0)
    c_iota = lax.broadcasted_iota(I32, (tokens_here, tokens_here), 1)
    ids_wide = jnp.broadcast_to(ids_row, (tokens_here, tokens_here))
    ids_col = jnp.sum(jnp.where(r_iota == c_iota, ids_wide, 0), axis=1, keepdims=True)
    same = ids_col == ids_row
    rank_row = jnp.sum(jnp.where(same & (r_iota < c_iota), 1, 0), axis=0, keepdims=True)
    rank_col = jnp.sum(jnp.where(same & (c_iota < r_iota), 1, 0), axis=1, keepdims=True)
    place_row, place_col = rank_row, rank_col
    far_row, far_col = jnp.zeros_like(ids_row), jnp.zeros_like(ids_col)
    for k, slot in enumerate(slots):
        to_dp, to_exp = peer(slot, 1)
        expert = to_dp * n_exp + to_exp
        place_row = place_row + jnp.where(ids_row == expert, off[k], 0)
        place_col = place_col + jnp.where(ids_col == expert, off[k], 0)
        if slot[1] and pooled:
            far_row = far_row + jnp.where(ids_row == expert, 1, 0)
            far_col = far_col + jnp.where(ids_col == expert, 1, 0)
    second_row, second_col = place_row + cap, place_col + cap
    if pooled:
        over_row = jnp.where(rank_row >= base, far_row, 0)
        over_col = jnp.where(rank_col >= base, far_col, 0)
        turn_row = jnp.sum(jnp.where(r_iota < c_iota, over_col, 0), axis=0, keepdims=True)
        turn_col = jnp.sum(jnp.where(c_iota < r_iota, over_row, 0), axis=1, keepdims=True)
        spill = jnp.sum(jnp.where(turn_row >= cap, over_row, 0), axis=1, keepdims=True)
        turn_row = jnp.where(turn_row >= cap, AWAY, turn_row)
        turn_col = jnp.where(turn_col >= cap, AWAY, turn_col)
        second_row = jnp.where(over_row == 1, turn_row + cap, place_row + jnp.where(far_row == 1, base, cap))
        second_col = jnp.where(over_col == 1, turn_col + cap, place_col + jnp.where(far_col == 1, base, cap))
        place_row = jnp.where(over_row == 1, turn_row, place_row)
        place_col = jnp.where(over_col == 1, turn_col, place_col)
        here = (turn_col == c_iota) | (turn_col + cap == c_iota)
        named = jnp.where((over_col == 1) & here, ids_col + 1, 0)
        my_pool_ids[...] = jnp.broadcast_to(
            jnp.sum(named, axis=0, keepdims=True).astype(F32), my_pool_ids.shape
        )

    fwd, back = [], []
    for k, slot in enumerate(slots):
        if k == own:
            fwd.append(None)
            back.append(None)
            continue
        fwd.append(remote(send.at[span(k)], recv.at[span(k)], fwd_send.at[k], fwd_recv.at[k],
                          at(peer(slot, 1))))
        back.append(remote(res.at[span(k)], ret.at[span(k)], ret_send.at[k], ret_recv.at[k],
                           at(peer(slot, -1))))
    hops, shares, parts = [], [], []
    more = 2 * (cap - base)
    if pooled:
        block = pl.ds(0, 2 * cap)
        across, home = at(peer((0, 1, 0), 1)), at(peer((0, 1, 0), -1))
        hops = [
            remote(send.at[block], pool, hop_send.at[0], hop_recv.at[0], across),
            remote(my_pool_ids, pool_ids, hop_send.at[1], hop_recv.at[1], across),
            remote(res.at[block], ret.at[block], hop_send.at[2], hop_recv.at[2], home),
        ]
        for j, slot in enumerate(slots[:n_near]):
            if j == own:
                continue
            cut = pl.ds(j * more, more)
            shares.append(remote(spread.at[cut], extra.at[cut], share_send.at[j], share_recv.at[j],
                                 at(peer(slot, 1))))
            parts.append(remote(extra_out.at[cut], extra_in.at[cut], part_send.at[j], part_recv.at[j],
                                at(peer(slot, -1))))

    def pack(first, last):
        spot = lax.broadcasted_iota(I32, (last - first, tokens_here), 0) + first
        pick_tok = jnp.where(spot == place_row, 1.0, 0.0).astype(BF16)
        pick_cot = jnp.where(spot == second_row, 1.0, 0.0).astype(BF16)
        pick = jnp.concatenate([pick_tok, pick_cot], axis=1)
        send[first:last] = jnp.dot(pick, stacked[...], preferred_element_type=F32).astype(BF16)

    loads[0].wait()
    loads[1].wait()
    edges = [n_near, n_near + n_far_a, count]
    groups = [(n_near, edges[1]), (0, n_near), (edges[1], count)]
    waited = False
    if pooled:
        pack(0, 2 * cap)
        pl.semaphore_wait(barrier, count - 1 + n_ctx - 1)
        waited = True
        hops[1].start()
        hops[0].start()
    for first, last in groups:
        if first == last:
            continue
        pack(off[first], off[last - 1] + size[last - 1])
        if not waited:
            pl.semaphore_wait(barrier, count - 1 + n_ctx - 1)
            waited = True
        for k in range(first, last):
            if k != own:
                fwd[k].start()

    row_e = lax.broadcasted_iota(I32, (experts, width), 0)
    router_row = jnp.sum(jnp.where(row_e == me, rw[...].astype(F32), 0.0), axis=0, keepdims=True)

    def expert_pass(x_wide, c_wide, use_term):
        m = x_wide.shape[0]
        x = x_wide.astype(BF16)
        logits = lax.dot_general(x, rw[...], NT, preferred_element_type=F32)
        lane = lax.broadcasted_iota(I32, (m, experts), 1)
        gate = jax.nn.sigmoid(jnp.sum(jnp.where(lane == me, logits, 0.0), axis=1, keepdims=True))
        upstream = (gate * c_wide).astype(BF16)
        pre = jnp.dot(x, gu[...], preferred_element_type=F32)
        a = pre[:, :hidden_units]
        u = pre[:, hidden_units:]
        s = jax.nn.sigmoid(a)
        act = a * s
        hidden = (act * u).astype(BF16)
        out = jnp.dot(hidden, dn[...], preferred_element_type=F32).astype(BF16).astype(F32)
        agreement = jnp.sum(c_wide * out, axis=1, keepdims=True)
        dense = (gate * (1.0 - gate) * agreement).astype(BF16).astype(F32)
        use_term(jnp.sum(dense * x_wide, axis=0, keepdims=True))
        moe = gate * out
        back_hidden = lax.dot_general(upstream, dn[...], NT, preferred_element_type=F32)
        back_pre = jnp.concatenate(
            [back_hidden * u * (s * (1.0 + a * (1.0 - s))), back_hidden * act], axis=1
        ).astype(BF16)
        back_in = lax.dot_general(back_pre, gu[...], NT, preferred_element_type=F32)
        grad = back_in.astype(BF16).astype(F32) + dense * router_row
        return moe, grad

    def slots_pass(first, last, use_term, with_extra=False, ready=None):
        xs, cs = [], []
        for k in range(first, last):
            if k == own:
                block = send[span(k)].astype(F32)
            else:
                fwd[k].wait_recv()
                block = recv[span(k)].astype(F32)
            xs.append(block[:size[k] // 2])
            cs.append(block[size[k] // 2:])
        if with_extra:
            for share in shares:
                share.wait_recv()
            for j in range(n_near):
                source = spread if j == own else extra
                block = source[j * more:(j + 1) * more].astype(F32)
                xs.append(block[:more // 2])
                cs.append(block[more // 2:])
        moe, grad = expert_pass(jnp.concatenate(xs, axis=0), jnp.concatenate(cs, axis=0), use_term)
        start = 0
        if with_extra:
            start = (last - first) * size[first] // 2
            for j in range(n_near):
                part = slice(start + j * more // 2, start + (j + 1) * more // 2)
                target = extra_in if j == own else extra_out
                target[j * more:(j + 1) * more] = jnp.concatenate([moe[part], grad[part]], axis=0).astype(BF16)
            for copy in parts:
                copy.start()
        each = size[first] // 2
        for i, k in enumerate(range(first, last)):
            part = slice(i * each, (i + 1) * each)
            block = jnp.concatenate([moe[part], grad[part]], axis=0).astype(BF16)
            if k == own:
                ret[span(k)] = block
            else:
                res[span(k)] = block
                if k == first and ready is not None:
                    ready()
                back[k].start()

    if pooled:
        hops[1].wait_recv()
        hops[0].wait_recv()
        wide = 2 * cap
        pr = lax.broadcasted_iota(I32, (wide, wide), 0)
        pc = lax.broadcasted_iota(I32, (wide, wide), 1)
        name_row = pool_ids[0:1, 0:wide]
        name_col = jnp.sum(jnp.where(pr == pc, jnp.broadcast_to(name_row, (wide, wide)), 0.0), axis=1, keepdims=True)
        lane, line = pc[0:1, :], pr[:, 0:1]
        mate = (name_col == name_row) & ((pr >= cap) == (pc >= cap))
        to_row = jnp.sum(jnp.where(mate & (pr < pc), 1, 0), axis=0, keepdims=True)
        to_col = jnp.sum(jnp.where(mate & (pc < pr), 1, 0), axis=1, keepdims=True)
        to_row = to_row + jnp.where(lane >= cap, more // 2, 0) + jnp.where(name_row == 0.0, AWAY, 0)
        to_col = to_col + jnp.where(line >= cap, more // 2, 0) + jnp.where(name_col == 0.0, AWAY, 0)
        for j, slot in enumerate(slots[:n_near]):
            to_dp, to_exp = peer(slot, 1)
            expert = (to_dp * n_exp + to_exp + 1).astype(F32)
            to_row = to_row + jnp.where(name_row == expert, j * more, 0)
            to_col = to_col + jnp.where(name_col == expert, j * more, 0)
        spot = lax.broadcasted_iota(I32, (n_near * more, wide), 0)
        deal = jnp.where(spot == to_row, 1.0, 0.0).astype(BF16)
        spread[...] = jnp.dot(deal, pool[...], preferred_element_type=F32).astype(BF16)
        for share in shares:
            share.start()
    loads[2].wait()
    loads[3].wait()
    router_terms = []
    tiny = []

    def scatter_column(term):
        router_sum = term
        for other in router_terms:
            router_sum = router_sum + other
        router_sum = router_sum * (1.0 / total)
        for q in range(n_ctx):
            for r in range(per):
                start = (q * per + r) * 128
                mine[q, r:r + 1, :] = router_sum[:, start:start + 128]
            if pooled:
                mine[q, per:per + 1, :] = jnp.broadcast_to(spill.astype(F32), (1, 128))
        for j in range(1, n_ctx):
            to = lax.rem(me_ctx + j, n_ctx)
            tiny.append(remote(mine.at[to], terms.at[me_ctx], ctx_send.at[j], ctx_recv.at[me_ctx], at_ctx(to)))
            tiny[-1].start()

    def send_column():
        column = mine[me_ctx]
        for j in range(1, n_ctx):
            source = lax.rem(me_ctx + j, n_ctx)
            remote(mine.at[source], terms.at[source], ctx_send.at[j], ctx_recv.at[source], at_ctx(source)).wait_recv()
            column = column + terms[source]
        summed[...] = column
        columns[me_ctx, me] = column
        for k, slot in list(enumerate(slots))[::-1]:
            if k != own:
                tiny.append(remote(summed, columns.at[me_ctx, me], col_send.at[k], col_recv.at[me], at(peer(slot, 1))))
                tiny[-1].start()

    keep, n_last = router_terms.append, (edges[1], count) if n_far_b else (0, n_near)
    if n_far_b:
        slots_pass(n_near, edges[1], keep)
        slots_pass(0, n_near, keep, pooled)
    else:
        slots_pass(n_near, edges[1], keep)
    if pooled:
        for part in parts:
            part.wait_recv()
        spot = lax.broadcasted_iota(I32, (wide, n_near * more), 1)
        gather = jnp.where(spot == to_col, 1.0, 0.0).astype(BF16)
        res[0:wide] = jnp.dot(gather, extra_in[...], preferred_element_type=F32).astype(BF16)
        hops[2].start()
    slots_pass(*n_last, scatter_column, ready=send_column)
    for k, slot in enumerate(slots):
        if k != own:
            from_dp, from_exp = peer(slot, -1)
            source = from_dp * n_exp + from_exp
            remote(summed, columns.at[me_ctx, source], col_send.at[k], col_recv.at[source],
                   at(peer(slot, -1))).wait_recv()
    for j in range(1, n_ctx):
        tiny.append(remote(columns.at[me_ctx], columns.at[me_ctx], all_send.at[j], all_recv.at[me_ctx],
                           at_ctx(lax.rem(me_ctx + j, n_ctx))))
        tiny[-1].start()

    def unpack(first, last, fresh):
        spot = lax.broadcasted_iota(I32, (tokens_here, last - first), 1) + first
        put_moe = jnp.where(spot == place_col, 1.0, 0.0).astype(BF16)
        put_grad = jnp.where(spot == second_col, 1.0, 0.0).astype(BF16)
        put = jnp.concatenate([put_moe, put_grad], axis=0)
        placed = jnp.dot(put, ret[first:last], preferred_element_type=F32)
        if fresh:
            moe_out[...] = placed[:tokens_here].astype(BF16)
            grad_out[...] = placed[tokens_here:].astype(BF16)
        else:
            moe_out[...] = (moe_out[...].astype(F32) + placed[:tokens_here]).astype(BF16)
            grad_out[...] = (grad_out[...].astype(F32) + placed[tokens_here:]).astype(BF16)

    split = edges[1] if n_far_b else count
    for k in range(split):
        if k != own:
            back[k].wait_recv()
    if pooled:
        hops[2].wait_recv()
    middle = off[split - 1] + size[split - 1]
    unpack(0, middle, True)
    if split < count:
        for k in range(split, count):
            back[k].wait_recv()
        unpack(middle, total_rows, False)

    for j in range(1, n_ctx):
        source = lax.rem(me_ctx + j, n_ctx)
        remote(columns.at[source], columns.at[source], all_send.at[j], all_recv.at[source],
               at_ctx(source)).wait_recv()
    for q in range(n_ctx):
        for r in range(per):
            start = (q * per + r) * 128
            rg_out[:, start:start + 128] = columns[q, :, r, :]
    if pooled:
        flag_out[0, 0] = jnp.where(jnp.max(columns[0, :, per, :]) > 0.0, 1, 0)
    else:
        flag_out[0, 0] = jnp.int32(0)
    for copy in fwd + back + hops + shares + parts:
        if copy is not None:
            copy.wait_send()
    for copy in tiny:
        copy.wait_send()


def hand_over(moe, grad, columns, moe_out, grad_out, rg_out, moe_buf, grad_buf, rg_buf, in_sem, out_sem):
    half = moe.shape[0] // 2
    parts = [(columns, rg_buf, rg_out)]
    for source, buffer, target in ((moe, moe_buf, moe_out), (grad, grad_buf, grad_out)):
        for start in (0, half):
            cut = pl.ds(start, half)
            parts.append((source.at[cut], buffer.at[cut], target.at[cut]))
    loads, stores = [], []
    for i, (source, buffer, target) in enumerate(parts):
        loads.append(pltpu.make_async_copy(source, buffer, in_sem.at[i]))
        stores.append(pltpu.make_async_copy(buffer, target, out_sem.at[i]))
    for load in loads:
        load.start()
    for load, store in zip(loads, stores):
        load.wait()
        store.start()
    for store in stores:
        store.wait()


def send_out(moe, grad, columns, moe_out, grad_out, rg_out, sem):
    half = moe.shape[0] // 2
    copies = [(columns, rg_out)]
    for source, target in ((moe, moe_out), (grad, grad_out)):
        for start in (0, half):
            cut = pl.ds(start, half)
            copies.append((source.at[cut], target.at[cut]))
    copies = [pltpu.make_async_copy(a, b, sem.at[i]) for i, (a, b) in enumerate(copies)]
    for copy in copies:
        copy.start()
    for copy in copies:
        copy.wait()


def exchange(shape, base, collective, tokens, cotangent, ids, router, gate_up, down_weight):
    n_dp, n_ctx, n_exp = shape
    tok_count, width = tokens.shape
    experts = router.shape[0]
    hidden_units = down_weight.shape[1]
    cap = capacity(tok_count, experts)
    slots, counts, _, _, total_rows, pooled = layout(n_dp, n_exp, cap, base)
    count, n_near = len(slots), counts[0]
    total = tok_count * n_dp * n_ctx * n_exp
    piece = -(-(width // 128 // n_ctx + 1) // 8) * 8
    vmem = pl.BlockSpec(memory_space=pltpu.VMEM)
    hbm = pl.BlockSpec(memory_space=pl.ANY)
    dma = pltpu.SemaphoreType.DMA
    rows = pltpu.VMEM((total_rows, width), BF16)
    more = pltpu.VMEM((n_near * 2 * (cap - base), width), BF16)
    names = pltpu.VMEM((8, 128), F32)
    scratch = [
        pltpu.VMEM((2 * tok_count, width), BF16),
        rows, rows, rows, rows,
        pltpu.VMEM((width, 2 * hidden_units), BF16),
        pltpu.VMEM((hidden_units, width), BF16),
        pltpu.VMEM((n_ctx, piece, 128), F32),
        pltpu.VMEM((piece, 128), F32),
        pltpu.VMEM((n_ctx, piece, 128), F32),
        pltpu.VMEM((n_ctx, experts, piece, 128), F32),
        dma((4,)),
        dma((count,)), dma((count,)), dma((count,)), dma((count,)),
        dma((n_ctx,)), dma((n_ctx,)),
        dma((count,)), dma((count,)),
        dma((n_ctx,)), dma((n_ctx,)),
    ]
    if pooled:
        scratch += [
            pltpu.VMEM((2 * cap, width), BF16), names, names, more, more, more, more,
            dma((3,)), dma((3,)), dma((n_near,)), dma((n_near,)), dma((n_near,)), dma((n_near,)),
        ]
    flops = 2 * 2 * count * cap * width * 3 * hidden_units
    return pl.pallas_call(
        functools.partial(kernel, n_dp, n_ctx, n_exp, cap, base, total),
        out_shape=(
            jax.ShapeDtypeStruct((tok_count, width), BF16),
            jax.ShapeDtypeStruct((tok_count, width), BF16),
            jax.ShapeDtypeStruct((experts, width), F32),
            jax.ShapeDtypeStruct((1, 1), I32),
        ),
        in_specs=[hbm, hbm, vmem, vmem, hbm, hbm],
        out_specs=(vmem, vmem, vmem, pl.BlockSpec(memory_space=pltpu.SMEM)),
        scratch_shapes=scratch,
        compiler_params=pltpu.CompilerParams(
            collective_id=collective, has_side_effects=True, vmem_limit_bytes=58 * 1024 * 1024
        ),
        cost_estimate=pl.CostEstimate(
            flops=flops, bytes_accessed=12 * 1024 * 1024, transcendentals=0
        ),
    )(tokens, cotangent, ids, router, gate_up, down_weight)


def deliver_now(moe, grad, columns):
    hbm = pl.BlockSpec(memory_space=pl.ANY)
    return pl.pallas_call(
        send_out,
        out_shape=tuple(jax.ShapeDtypeStruct(v.shape, v.dtype) for v in (moe, grad, columns)),
        in_specs=[hbm, hbm, hbm],
        out_specs=(hbm, hbm, hbm),
        scratch_shapes=[pltpu.SemaphoreType.DMA((5,))],
    )(moe, grad, columns)


def deliver(moe, grad, columns):
    hbm = pl.BlockSpec(memory_space=pl.ANY)
    dma = pltpu.SemaphoreType.DMA
    return pl.pallas_call(
        hand_over,
        out_shape=tuple(jax.ShapeDtypeStruct(v.shape, v.dtype) for v in (moe, grad, columns)),
        in_specs=[hbm, hbm, hbm],
        out_specs=(hbm, hbm, hbm),
        scratch_shapes=[
            pltpu.VMEM(moe.shape, BF16),
            pltpu.VMEM(grad.shape, BF16),
            pltpu.VMEM(columns.shape, F32),
            dma((5,)),
            dma((5,)),
        ],
    )(moe, grad, columns)


def capacity(tok_count, experts):
    most = min(tok_count, 3 * tok_count // (2 * experts))
    return -(-most // 8) * 8


def per_device(n_dp, n_ctx, n_exp, tokens, cotangent, expert_ids, router_weight, gate_up, down_weight):
    tok_count = tokens.shape[0]
    cap = capacity(tok_count, router_weight.shape[1])
    base = min(cap, -(-(2 * cap // 3) // 8) * 8)
    shape = (n_dp, n_ctx, n_exp)
    args = (tokens, cotangent, expert_ids.reshape(1, tok_count), router_weight.T, gate_up, down_weight)
    moe, grad, columns, spilled = exchange(shape, base, 0, *args)
    if base == cap:
        moe, grad, columns = deliver(moe, grad, columns)
        return moe, grad, columns.T

    def short(moe, grad, columns, *args):
        return deliver_now(moe, grad, columns)

    def full(moe, grad, columns, *args):
        return deliver(*exchange(shape, cap, 1, *args)[:3])

    moe, grad, columns = lax.switch(spilled[0, 0], (short, full), moe, grad, columns, *args)
    return moe, grad, columns.T


def solution(mesh):
    in_specs = (
        P(("dp", "ctx", "exp"), None),
        P(("dp", "ctx", "exp"), None),
        P(("dp", "ctx", "exp"), None),
        P(),
        P(("dp", "exp"), None, None),
        P(("dp", "exp"), None, None),
    )
    out_specs = (P(("dp", "ctx", "exp"), None), P(("dp", "ctx", "exp"), None), P())
    shape = mesh.shape
    return jax.shard_map(
        functools.partial(per_device, shape["dp"], shape["ctx"], shape["exp"]),
        mesh=mesh, in_specs=in_specs, out_specs=out_specs, check_vma=False,
    )
```
